256 devices in a mesh: layer: 64 (over y, z_lo, x), dp: 4 (over z_hi, core).
Axes of the slice: x: 4, y: 4, z: 8 (z_hi: 2, z_lo: 4; z = z_hi * 4 + z_lo), core: 2. Of those that a mesh axis runs over, the one named last changes fastest.
Arguments:
- images: float32 [8, 16, 16, 128], P('dp'), may hold values from -6 to 6
- weights: bfloat16 [256, 3, 3, 128, 128], P('layer'), may hold values from -0.1875 to 0.1875
- biases: float32 [256, 128], P('layer'), may hold values from -3 to 3
- end_grad: float32 [8, 16, 16, 128], P('dp'), may hold values from -6 to 6
Outputs:
- interval_ends: float32 [64, 8, 16, 16, 128], P('layer', 'dp')
- start_adjoint: float32 [64, 8, 16, 16, 128], P('layer', 'dp')
- weight_grad: float32 [256, 3, 3, 128, 128], P('layer')
- bias_grad: float32 [256, 128], P('layer')
The draws below stay inside these ranges and needn't reach their ends.
All inputs are finite; a program needn't handle non-finite values.
Results may differ from the reference program's by a relative error of at most 0.012.
The reference program's roundings to bfloat16 on the way count: a program that leaves them out, or rounds other values in their place, can miss the bound.
Values sent between devices are 32-bit elements; how exact they have to be, the bound alone decides.
No kernel may reach another device: no remote copies, remote signals or barrier semaphores. Data moves between devices by JAX's collectives and lax.ppermute only.
A program may use at most 128 MiB of HBM per device.

```python
import jax
import jax.numpy as jnp
from jax import lax

C = 128
H = 16
W = 16
BLK = 4
LAYERS = 256
IMAGES = 8
N_LAYER = 64


def steps_of(own_key, shape, split, least, high):
    loudness = 1.0
    for axis_at, blocks in split:
        draws = jax.random.uniform(jax.random.fold_in(jax.random.fold_in(own_key, 6), axis_at), (blocks,), jnp.float32, least / len(split), high / len(split))
        loudness = loudness * jnp.repeat(jnp.exp(draws), shape[axis_at] // blocks).reshape((-1,) + (1,) * (len(shape) - 1 - axis_at))
    return loudness


def noise(stream_key, shape, spread, limit, cuts=(), kind=jnp.bfloat16):
    loudness = steps_of(stream_key, shape, cuts, -0.22, 0.18) if cuts else 1.0
    drawn = jax.random.normal(stream_key, shape, jnp.float32) * spread * loudness
    return jnp.minimum(jnp.maximum(drawn, -limit), limit).astype(kind)


def setup_inputs(seed: int = 0) -> dict:
    arg_keys = jax.random.split(jax.random.key(seed), 5)
    return {
        "images": noise(arg_keys[0], (IMAGES, H, W, C), 1.0, 6.0, ((0, 4),), jnp.float32),
        "weights": noise(arg_keys[1], (LAYERS, 3, 3, C, C), (9 * C) ** -0.5, 0.1875, ((0, 64),)),
        "biases": noise(arg_keys[2], (LAYERS, C), 0.5, 3.0, ((0, 64),), jnp.float32),
        "end_grad": noise(arg_keys[3], (IMAGES, H, W, C), 1.0, 6.0, ((0, 4),), jnp.float32),
    }


step_size = 0.25
conv_layout = ('NHWC', 'HWIO', 'NHWC')

def convolve(states, kernel):
    return lax.conv_general_dilated(states.astype(jnp.bfloat16), kernel, (1, 1), 'SAME', dimension_numbers=conv_layout, preferred_element_type=jnp.float32)

def advance(states, weights, biases):
    inputs = []
    slopes = []
    for index in range(weights.shape[0]):
        preact = convolve(states, weights[index]) + biases[index]
        activation = jnp.tanh(preact)
        inputs.append(states.astype(jnp.bfloat16))
        slopes.append(activation)
        states = states + step_size * activation
    return (states, inputs, slopes)

def retreat(adjoint, transposed, slopes):
    for index in reversed(range(len(slopes))):
        change = step_size * (1.0 - slopes[index] * slopes[index]) * adjoint
        adjoint = adjoint + convolve(change, transposed[index])
    return adjoint

def kernel_grad(inputs_low, change_low):
    padded = jnp.pad(inputs_low, ((0, 0), (1, 1), (1, 1), (0, 0))).astype(jnp.float32)
    change_wide = change_low.astype(jnp.float32)
    height = change_low.shape[1]
    width = change_low.shape[2]
    taps = []
    for row_at in range(3):
        line = []
        for col_at in range(3):
            window = padded[:, row_at:row_at + height, col_at:col_at + width, :]
            line.append(jnp.einsum('bhwc,bhwd->cd', window, change_wide))
        taps.append(jnp.stack(line))
    return jnp.stack(taps)

def finish(adjoint, transposed, inputs, slopes):
    kernels = []
    offsets = []
    for index in reversed(range(len(slopes))):
        change = step_size * (1.0 - slopes[index] * slopes[index]) * adjoint
        change_low = change.astype(jnp.bfloat16)
        kernels.append(kernel_grad(inputs[index], change_low))
        offsets.append(lax.optimization_barrier(jnp.sum(change, axis=(0, 1, 2))))
        adjoint = adjoint + convolve(change_low, transposed[index])
    return (adjoint, jnp.stack(kernels[::-1]), jnp.stack(offsets[::-1]))

def coarse_chain(matrices, residues, backward):

    def advance_error(carried, pieces):
        matrix, residue = pieces
        return (jnp.einsum('bhwc,cd->bhwd', carried, matrix, precision=lax.Precision.HIGHEST) + residue, carried)
    _, result = lax.scan(advance_error, jnp.zeros_like(residues[0]), (matrices, residues), reverse=backward)
    return result

def apply_map(field, matrix):
    return jnp.einsum('bhwc,cd->bhwd', field, matrix, precision=lax.Precision.HIGHEST)

def reference(images, weights, biases, end_grad):
    kernels = weights.reshape(N_LAYER, BLK, 3, 3, C, C)
    offsets = biases.reshape(N_LAYER, BLK, C)
    transposed = jnp.swapaxes(jnp.flip(kernels, (2, 3)), 4, 5)
    matrices = jnp.eye(C, dtype=jnp.float32) + step_size * lax.optimization_barrier(jnp.sum(kernels[:, :, 1, 1].astype(jnp.float32), axis=1))
    guess = jax.vmap(apply_map, in_axes=(None, 0))(images, matrices)
    starts = jnp.concatenate([images[None], guess[:-1]], axis=0)
    relaxed, _, _ = jax.vmap(advance, in_axes=(0, 0, 0))(starts, kernels, offsets)
    error = coarse_chain(matrices, relaxed - guess, False)
    corrected = starts + error
    interval_ends, inputs, slopes = jax.vmap(advance, in_axes=(0, 0, 0))(corrected, kernels, offsets)
    back = jax.vmap(apply_map, in_axes=(None, 0))(end_grad, jnp.swapaxes(matrices, 1, 2))
    ends_adj = jnp.concatenate([back[1:], end_grad[None]], axis=0)
    again = jax.vmap(retreat, in_axes=(0, 0, 0))(ends_adj, transposed, slopes)
    adj_error = coarse_chain(jnp.swapaxes(matrices, 1, 2), again - back, True)
    start_adjoint, kernel_sums, offset_sums = jax.vmap(finish, in_axes=(0, 0, 0, 0))(ends_adj + adj_error, transposed, inputs, slopes)
    divisor = 1.0 / images.shape[0]
    weight_grad = kernel_sums.reshape(LAYERS, 3, 3, C, C) * divisor
    bias_grad = offset_sums.reshape(LAYERS, C) * divisor
    return (interval_ends, start_adjoint, weight_grad, bias_grad)
```

```python
import jax
import jax.numpy as jnp
from jax import lax
from jax.experimental import pallas as pl
from jax.experimental.pallas import tpu as pltpu
from jax.sharding import PartitionSpec as P

GROUP = 8
VMEM_LIMIT = 48 * 1024 * 1024
f32 = jnp.float32
bf16 = jnp.bfloat16


def shifted_columns(value, width):
    rows = value.shape[0]
    at = lax.broadcasted_iota(jnp.int32, value.shape, 0) % width
    left = jnp.where(at == 0, 0.0, pltpu.roll(value, 1, 0))
    right = jnp.where(at == width - 1, 0.0, pltpu.roll(value, rows - 1, 0))
    return jnp.concatenate([left.astype(bf16), value.astype(bf16), right.astype(bf16)], axis=1)


def clear_border(ref):
    height = ref.shape[1]
    edge = jnp.zeros((ref.shape[0], 1) + ref.shape[2:], ref.dtype)
    ref[:, 0:1] = edge
    ref[:, height - 1 : height] = edge


def rows_from(ref, row_at):
    images, height, width, lanes = ref.shape
    return ref[:, row_at : row_at + height - 2].reshape(images * (height - 2) * width, lanes)


def convolve(ref, value, kernel):
    images, height, width, lanes = ref.shape
    ref[:, 1 : height - 1] = shifted_columns(value, width).reshape(images, height - 2, width, lanes)
    total = None
    for row_at in range(3):
        part = jnp.dot(
            rows_from(ref, row_at),
            kernel[row_at * lanes : (row_at + 1) * lanes],
            preferred_element_type=f32,
        )
        total = part if total is None else total + part
    return total


def split(value):
    high = value.astype(bf16)
    low = (value - high.astype(f32)).astype(bf16)
    return high, low


def times(value, matrix, transpose=False):
    dims = (((1,), (1 if transpose else 0,)), ((), ()))
    high, low = split(value)
    mhigh, mlow = split(matrix)
    dot = lambda a, b: lax.dot_general(a, b, dims, preferred_element_type=f32)
    return dot(high, mhigh) + (dot(low, mhigh) + dot(high, mlow))


def call(body, outs, *args, scratch=(), flops=0, name=None):
    vmem = pl.BlockSpec(memory_space=pltpu.VMEM)
    smem = pl.BlockSpec(memory_space=pltpu.SMEM)
    size = sum(a.size * a.dtype.itemsize for a in args)
    size += sum(o.size * o.dtype.itemsize for o in outs)
    return pl.pallas_call(
        body,
        out_shape=tuple(outs),
        in_specs=[smem if a.dtype == jnp.int32 else vmem for a in args],
        out_specs=tuple(vmem for _ in outs),
        scratch_shapes=list(scratch),
        cost_estimate=pl.CostEstimate(flops=flops, bytes_accessed=size, transcendentals=0),
        compiler_params=pltpu.CompilerParams(vmem_limit_bytes=VMEM_LIMIT),
        name=name,
    )(*args)


def shape(dims, dtype=f32):
    return jax.ShapeDtypeStruct(dims, dtype)


def coarse_body(centre, out):
    total = centre[0].astype(f32)
    for index in range(1, centre.shape[0]):
        total = total + centre[index].astype(f32)
    out[...] = 0.25 * total


def transpose_body(weights, out):
    taps, channels = weights.shape[1], weights.shape[2]
    for index in range(weights.shape[0]):
        for tap in range(taps):
            flipped = weights[index, taps - 1 - tap].astype(f32).T
            out[index, tap * channels : (tap + 1) * channels] = flipped.astype(bf16)


def start_body(images, own, before, weights, biases, starts_out, residual_out, ref):
    clear_border(ref)
    field = images[...]
    starts = field + times(field, before[...])
    starts_out[...] = starts
    state = starts
    for index in range(weights.shape[0]):
        state = state + 0.25 * jnp.tanh(
            convolve(ref, state, weights.at[index]) + biases[index : index + 1]
        )
    residual_out[...] = state - (field + times(field, own[...]))


def ends_body(end_grad, own, after, ends_out, back_out):
    field = end_grad[...]
    ends_out[...] = field + times(field, after[...], True)
    back_out[...] = field + times(field, own[...], True)


def product_body(group, out):
    total = group[0]
    for index in range(1, group.shape[0]):
        total = total + (group[index] + times(total, group[index]))
    out[...] = total


def order(backward):
    return range(GROUP - 1, -1, -1) if backward else range(GROUP)


def total_body(backward, pieces, group, out):
    error = None
    for index in order(backward):
        if error is None:
            error = pieces[index]
        else:
            error = error + (times(error, group[index], backward) + pieces[index])
    out[...] = error


def replay_body(backward, mine, totals, products, pieces, group, out):
    error = jnp.zeros(totals.shape[1:], f32)
    for index in list(order(backward))[:-1]:
        longer = error + (times(error, products[index], backward) + totals[index])
        use = mine[0] < index if backward else mine[0] > index
        error = jnp.where(use, longer, error)
    for index in order(backward):
        out[index] = error
        if index != order(backward)[-1]:
            error = error + (times(error, group[index], backward) + pieces[index])


def forward_sweep(state, weights, biases, ref, inputs_out, slopes_out):
    for index in range(weights.shape[0]):
        activation = jnp.tanh(convolve(ref, state, weights.at[index]) + biases[index : index + 1])
        channels = state.shape[1]
        inputs_out[index] = ref[:, :, :, channels : 2 * channels]
        slopes_out[index] = 0.25 * (1.0 - activation * activation)
        state = state + 0.25 * activation
    return state


def middle_body(
    starts, error, ends_adj, back, weights, biases, transposed,
    corrected_out, ends_out, inputs_out, slopes_out, residual_out, ref,
):
    clear_border(ref)
    corrected = starts[...] + error[...]
    corrected_out[...] = corrected
    ends_out[...] = forward_sweep(corrected, weights, biases, ref, inputs_out, slopes_out)
    adjoint = ends_adj[...]
    for index in reversed(range(weights.shape[0])):
        change = slopes_out[index] * adjoint
        adjoint = adjoint + convolve(ref, change, transposed.at[index])
    residual_out[...] = adjoint - back[...]


def again_body(corrected, weights, biases, inputs_out, slopes_out, ref):
    clear_border(ref)
    forward_sweep(corrected[...], weights, biases, ref, inputs_out, slopes_out)


def finish_block(scale, adjoint, transposed, inputs, slope, ref):
    channels = adjoint.shape[1]
    change = slope * adjoint
    adjoint = adjoint + convolve(ref, change, transposed)
    offset = jnp.sum(change, axis=0, keepdims=True) * scale
    moved = rows_from(ref, 1)
    field = jnp.concatenate([rows_from(inputs, row_at) for row_at in range(3)], axis=1)
    kernel = scale * lax.dot_general(
        field, moved, (((0,), (0,)), ((), ())), preferred_element_type=f32
    )
    taps = [
        kernel[
            row_at * channels : (row_at + 1) * channels,
            (2 - col_at) * channels : (3 - col_at) * channels,
        ]
        for row_at in range(3)
        for col_at in range(3)
    ]
    return adjoint, taps, offset


def final_body(
    scale, ends_adj, error, transposed, inputs, slopes, adjoint_out, kernels_out, offsets_out, ref
):
    clear_border(ref)
    adjoint = ends_adj[...] + error[...]
    for index in reversed(range(transposed.shape[0])):
        adjoint, taps, offset = finish_block(
            scale, adjoint, transposed.at[index], inputs.at[index], slopes[index], ref
        )
        for tap in range(9):
            kernels_out[index, tap] = taps[tap]
        offsets_out[index : index + 1] = offset
    adjoint_out[...] = adjoint


def final_add_body(
    scale, ends_adj, error, transposed, inputs, slopes, kernels, offsets,
    kernels_out, offsets_out, ref,
):
    clear_border(ref)
    adjoint = ends_adj[...] + error[...]
    for index in reversed(range(transposed.shape[0])):
        adjoint, taps, offset = finish_block(
            scale, adjoint, transposed.at[index], inputs.at[index], slopes[index], ref
        )
        for tap in range(9):
            kernels_out[index, tap] = kernels[index, tap] + taps[tap]
        offsets_out[index : index + 1] = offsets[index : index + 1] + offset


def shards(images, weights, biases, end_grad):
    count, height, width, channels = images.shape
    blocks = weights.shape[0]
    rows = count * height * width
    layers = lax.axis_size("layer")
    outer = layers // GROUP
    near = [[a * GROUP + b for b in range(GROUP)] for a in range(outer)]
    far = [[a * GROUP + b for a in range(outer)] for b in range(GROUP)]
    dp = lax.axis_size("dp")
    partner = [(i, (i + dp // 2) % dp) for i in range(dp)]
    sibling = [(i, i ^ 1) for i in range(dp)]
    mine = (lax.axis_index("layer") // GROUP).astype(jnp.int32).reshape(1)
    scale = 1.0 / (count * dp)
    per_conv = 2 * rows * 9 * channels * channels

    def exchange(value, groups):
        return lax.all_to_all(value, "layer", 0, 0, axis_index_groups=groups)

    flat = weights.reshape(blocks, 9, channels, channels)
    kernels = weights.reshape(blocks, 9 * channels, channels)
    field = images.reshape(rows, channels)
    cotangent = end_grad.reshape(rows, channels)
    matrix_shape = (channels, channels)
    ref = pltpu.VMEM((count, height + 2, width, 3 * channels), bf16)

    (own,) = call(coarse_body, [shape(matrix_shape)], flat[:, 4], name="coarse")
    before = lax.ppermute(own, "layer", [(i, i + 1) for i in range(layers - 1)])
    after = lax.ppermute(own, "layer", [(i + 1, i) for i in range(layers - 1)])
    group = exchange(jnp.broadcast_to(own, (GROUP,) + matrix_shape), near)
    (transposed,) = call(
        transpose_body, [shape((blocks, 9 * channels, channels), bf16)], flat, name="flip"
    )

    starts, residual = call(
        start_body, [shape((rows, channels))] * 2, field, own, before, kernels, biases,
        scratch=[ref], flops=blocks * per_conv, name="start",
    )
    ends_adj, back = call(
        ends_body, [shape((rows, channels))] * 2, cotangent, own, after, name="ends"
    )
    (product,) = call(product_body, [shape(matrix_shape)], group, name="product")
    products = exchange(jnp.broadcast_to(product, (outer,) + matrix_shape), far)

    def scan(residual, backward):
        part = rows // GROUP
        pieces = exchange(residual.reshape(GROUP, part, channels), near)
        (total,) = call(
            lambda *refs: total_body(backward, *refs), [shape((part, channels))], pieces, group,
            name="total",
        )
        totals = exchange(jnp.broadcast_to(total, (outer, part, channels)), far)
        (error,) = call(
            lambda *refs: replay_body(backward, *refs), [shape((GROUP, part, channels))],
            mine, totals, products, pieces, group, name="replay",
        )
        return exchange(error, near).reshape(rows, channels)

    inputs_shape = shape((blocks, count, height + 2, width, channels), bf16)
    slopes_shape = shape((blocks, rows, channels))
    error = scan(residual, False)
    corrected, interval_ends, inputs, slopes, adj_residual = call(
        middle_body,
        [shape((rows, channels))] * 2 + [inputs_shape, slopes_shape, shape((rows, channels))],
        starts, error, ends_adj, back, kernels, biases, transposed,
        scratch=[ref], flops=2 * blocks * per_conv, name="middle",
    )
    other_corrected = lax.ppermute(corrected, "dp", partner)
    other_ends = lax.ppermute(ends_adj, "dp", partner)
    adj_error = scan(adj_residual, True)
    other_inputs, other_slopes = call(
        again_body, [inputs_shape, slopes_shape], other_corrected, kernels, biases,
        scratch=[ref], flops=blocks * per_conv, name="again",
    )
    other_error = lax.ppermute(adj_error, "dp", partner)
    kernels_shape = shape((blocks, 9, channels, channels))
    offsets_shape = shape((blocks, channels))
    adjoint, kernel_part, offset_part = call(
        lambda *refs: final_body(scale, *refs),
        [shape((rows, channels)), kernels_shape, offsets_shape],
        ends_adj, adj_error, transposed, inputs, slopes,
        scratch=[ref], flops=2 * blocks * per_conv, name="final",
    )
    kernel_part, offset_part = call(
        lambda *refs: final_add_body(scale, *refs), [kernels_shape, offsets_shape],
        other_ends, other_error, transposed, other_inputs, other_slopes, kernel_part, offset_part,
        scratch=[ref], flops=2 * blocks * per_conv, name="other",
    )
    weight_grad = kernel_part + lax.ppermute(kernel_part, "dp", sibling)
    bias_grad = offset_part + lax.ppermute(offset_part, "dp", sibling)
    full = (1, count, height, width, channels)
    return (
        interval_ends.reshape(full),
        adjoint.reshape(full),
        weight_grad.reshape(blocks, 3, 3, channels, channels),
        bias_grad,
    )


def solution(mesh):
    in_specs = (
        P("dp", None, None, None),
        P("layer", None, None, None, None),
        P("layer", None),
        P("dp", None, None, None),
    )
    out_specs = (
        P("layer", "dp", None, None, None),
        P("layer", "dp", None, None, None),
        P("layer", None, None, None, None),
        P("layer", None),
    )
    return jax.shard_map(shards, mesh=mesh, in_specs=in_specs, out_specs=out_specs, check_vma=False)
```

```python
import math

import jax
import jax.numpy as jnp
from jax import lax
from jax.experimental import pallas as pl
from jax.experimental.pallas import tpu as pltpu
from jax.sharding import PartitionSpec as P

GROUP = 8
EXTRA = 8
VMEM_LIMIT = 12 * 1024 * 1024
f32 = jnp.float32
bf16 = jnp.bfloat16


def shifted_columns(value, width):
    rows = value.shape[0]
    at = lax.broadcasted_iota(jnp.int32, value.shape, 0) % width
    left = jnp.where(at == 0, 0.0, pltpu.roll(value, 1, 0))
    right = jnp.where(at == width - 1, 0.0, pltpu.roll(value, rows - 1, 0))
    return jnp.concatenate([left.astype(bf16), value.astype(bf16), right.astype(bf16)], axis=1)


def clear_border(ref):
    height = ref.shape[1]
    edge = jnp.zeros((ref.shape[0], 1) + ref.shape[2:], ref.dtype)
    ref[:, 0:1] = edge
    ref[:, height - 1 : height] = edge


def rows_from(ref, row_at):
    images, height, width, lanes = ref.shape
    return ref[:, row_at : row_at + height - 2].reshape(images * (height - 2) * width, lanes)


def convolve(ref, value, kernel):
    images, height, width, lanes = ref.shape
    ref[:, 1 : height - 1] = shifted_columns(value, width).reshape(images, height - 2, width, lanes)
    total = None
    for row_at in range(3):
        part = jnp.dot(
            rows_from(ref, row_at),
            kernel[row_at * lanes : (row_at + 1) * lanes],
            preferred_element_type=f32,
        )
        total = part if total is None else total + part
    return total


def split(value):
    high = value.astype(bf16)
    low = (value - high.astype(f32)).astype(bf16)
    return high, low


def times(value, matrix, transpose=False):
    dims = (((1,), (1 if transpose else 0,)), ((), ()))
    high, low = split(value)
    mhigh, mlow = split(matrix)
    dot = lambda a, b: lax.dot_general(a, b, dims, preferred_element_type=f32)
    return dot(high, mhigh) + (dot(low, mhigh) + dot(high, mlow))


VMEM = pl.BlockSpec(memory_space=pltpu.VMEM)
SMEM = pl.BlockSpec(memory_space=pltpu.SMEM)
HBM = pl.BlockSpec(memory_space=pltpu.HBM)


def call(body, outs, *args, ins=None, out_specs=None, scratch=(), flops=0, aliases=None, name=None):
    size = sum(a.size * a.dtype.itemsize for a in args)
    size += sum(math.prod(o.shape) * jnp.dtype(o.dtype).itemsize for o in outs)
    return pl.pallas_call(
        body,
        out_shape=tuple(outs),
        in_specs=list(ins) if ins else [VMEM] * len(args),
        out_specs=tuple(out_specs) if out_specs else (VMEM,) * len(outs),
        scratch_shapes=list(scratch),
        input_output_aliases=aliases or {},
        cost_estimate=pl.CostEstimate(flops=flops, bytes_accessed=size, transcendentals=0),
        compiler_params=pltpu.CompilerParams(vmem_limit_bytes=VMEM_LIMIT),
        name=name,
    )(*args)


def shape(dims, dtype=f32):
    return pltpu.VMEM(dims, dtype)


def stored(dims, dtype=f32):
    return pltpu.HBM(dims, dtype)


def in_hbm(value):
    return pltpu.with_memory_space_constraint(value, pltpu.HBM)


def coarse_body(weights, out, centre, sem):
    copy = pltpu.make_async_copy(weights.at[:, 4], centre, sem)
    copy.start()
    copy.wait()
    total = centre[0].astype(f32)
    for index in range(1, centre.shape[0]):
        total = total + centre[index].astype(f32)
    out[...] = 0.25 * total


def load_body(
    weights, images, biases, end_grad, weights_out, images_out, biases_out, end_out, sems
):
    pairs = [(weights, weights_out), (images, images_out), (biases, biases_out)]
    pairs.append((end_grad, end_out))
    copies = [pltpu.make_async_copy(a, b, sems.at[at]) for at, (a, b) in enumerate(pairs)]
    for copy in copies:
        copy.start()
    for copy in copies:
        copy.wait()


def flip_body(weights, transposed):
    taps, channels = weights.shape[1], weights.shape[2]
    for index in range(weights.shape[0]):
        for tap in range(taps):
            flipped = weights[index, taps - 1 - tap].astype(f32).T
            transposed[index, tap * channels : (tap + 1) * channels] = flipped.astype(bf16)


def start_body(images, own, before, weights, biases, payload, ref):
    clear_border(ref)
    field = images[...]
    state = field + times(field, before[...])
    for index in range(weights.shape[0]):
        state = state + 0.25 * jnp.tanh(
            convolve(ref, state, weights.at[index]) + biases[index : index + 1]
        )
    matrix = own[...]
    residual = state - (field + times(field, matrix))
    part = residual.shape[0] // GROUP
    for index in range(GROUP):
        payload[index, :part] = residual[index * part : (index + 1) * part]
        payload[index, part:] = matrix


def ends_body(images, end_grad, own, before, after, starts_out, ends_out, back_out):
    field = images[...]
    starts_out[...] = field + times(field, before[...])
    field = end_grad[...]
    ends_out[...] = field + times(field, after[...], True)
    back_out[...] = field + times(field, own[...], True)


def total_body(pieces, payload, locals_out):
    part = locals_out.shape[1]
    error = pieces[0, :part]
    product = pieces[0, part:]
    for index in range(1, GROUP):
        matrix = pieces[index, part:]
        locals_out[index] = error
        error = error + (times(error, matrix) + pieces[index, :part])
        product = product + (matrix + times(product, matrix))
    payload[:part] = error
    payload[part:] = product


def pair_body(part, spot, mine, theirs, out):
    upper = spot[1] == 1
    early = jnp.where(upper, theirs[...], mine[...])
    late = jnp.where(upper, mine[...], theirs[...])
    out[...] = early + (times(early, late[part:]) + late)


def back_pair_body(part, spot, mine, theirs, mine_full, theirs_full, out):
    upper = spot[1] == 1
    early = jnp.where(upper, mine[...], theirs[...])
    late = jnp.where(upper, theirs[...], mine[...])
    matrix = jnp.where(upper, theirs_full[part:], mine_full[part:])
    out[...] = early + (times(early, matrix, True) + late)


def products_body(part, pieces, prefix_out, suffix_out):
    before = pieces[0, part:]
    after = pieces[GROUP - 1, part:]
    for index in range(1, GROUP):
        prefix_out[index] = before
        suffix_out[GROUP - 1 - index] = after
        if index < GROUP - 1:
            matrix = pieces[index, part:]
            before = before + (matrix + times(before, matrix))
            matrix = pieces[GROUP - 1 - index, part:]
            after = after + (matrix + times(matrix, after))


def back_total_body(part, pieces, first, payload, locals_out):
    error = pieces[GROUP - 1]
    for index in range(GROUP - 2, -1, -1):
        locals_out[index] = error
        error = error + (times(error, first[index, part:], True) + pieces[index])
    payload[...] = error


def replay_body(spot, theirs, far1, far2, far3, locals_in, prefix_in, out, prefix, sem):
    copy = pltpu.make_async_copy(prefix_in, prefix, sem)
    copy.start()
    part = out.shape[1]
    error = jnp.where(spot[0] >= 3, far3[:part], 0.0)
    for distance, group in ((2, far2), (1, far1)):
        longer = error + (times(error, group[part:]) + group[:part])
        error = jnp.where(spot[0] >= distance, longer, error)
    longer = error + (times(error, theirs[part:]) + theirs[:part])
    error = jnp.where(spot[1] == 1, longer, error)
    out[0] = error
    copy.wait()
    for index in range(1, GROUP):
        out[index] = error + (times(error, prefix[index]) + locals_in[index])


def back_replay_body(
    spot, theirs, far1, far2, far3, theirs_full, full1, full2, locals_in, suffix_in,
    out, suffix, sem,
):
    copy = pltpu.make_async_copy(suffix_in, suffix, sem)
    copy.start()
    part = out.shape[1]
    error = far3[...]
    for group, full in ((far2, full2), (far1, full1)):
        error = error + (times(error, full[part:], True) + group[...])
    longer = error + (times(error, theirs_full[part:], True) + theirs[...])
    error = jnp.where(spot[1] == 0, longer, error)
    out[GROUP - 1] = error
    copy.wait()
    for index in range(GROUP - 1):
        out[index] = error + (times(error, suffix[index], True) + locals_in[index])


def forward_sweep(state, weights, biases, ref, inputs, slopes, stores, fetches=None):
    for index in range(weights.shape[0]):
        if fetches is not None:
            fetches[index].wait()
        activation = jnp.tanh(convolve(ref, state, weights.at[index]) + biases[index : index + 1])
        channels = state.shape[1]
        inputs[index] = ref[:, :, :, channels : 2 * channels]
        slopes[index] = 0.25 * (1.0 - activation * activation)
        for store in stores[index]:
            store.start()
        state = state + 0.25 * activation
    return state


def sweep_stores(inputs, slopes, inputs_out, slopes_out, sems):
    blocks = inputs.shape[0]
    return [
        [
            pltpu.make_async_copy(inputs.at[index], inputs_out.at[index], sems.at[index]),
            pltpu.make_async_copy(slopes.at[index], slopes_out.at[index], sems.at[blocks + index]),
        ]
        for index in range(blocks)
    ]


def middle_body(
    error, starts_in, ends_in, back_in, weights_in, transposed_in, biases_in,
    corrected_out, ends_out, inputs_out, slopes_out, residual_out,
    ref, corrected, ends, inputs, slopes, starts, ends_adj, back, weights, transposed, biases,
    sems, loads,
):
    blocks = weights.shape[0]
    pairs = [(starts_in, starts), (biases_in, biases)]
    pairs += [(weights_in.at[index], weights.at[index]) for index in range(blocks)]
    pairs += [(transposed_in, transposed), (ends_in, ends_adj), (back_in, back)]
    fetches = [pltpu.make_async_copy(a, b, loads.at[at]) for at, (a, b) in enumerate(pairs)]
    for fetch in fetches:
        fetch.start()
    clear_border(ref)
    stores = sweep_stores(inputs, slopes, inputs_out, slopes_out, sems)
    fetches[0].wait()
    fetches[1].wait()
    corrected[...] = starts[...] + error[...]
    first = pltpu.make_async_copy(corrected, corrected_out, sems.at[2 * blocks])
    first.start()
    ends[...] = forward_sweep(
        corrected[...], weights, biases, ref, inputs, slopes, stores, fetches[2 : 2 + blocks]
    )
    for fetch in fetches[2 + blocks :]:
        fetch.wait()
    last = pltpu.make_async_copy(ends, ends_out, sems.at[2 * blocks + 1])
    last.start()
    adjoint = ends_adj[...]
    for index in reversed(range(blocks)):
        change = slopes[index] * adjoint
        adjoint = adjoint + convolve(ref, change, transposed.at[index])
    residual_out[...] = adjoint - back[...]
    for store in sum(stores, [first, last]):
        store.wait()


def again_body(corrected, weights, biases, inputs_out, slopes_out, ref, inputs, slopes, sems):
    clear_border(ref)
    stores = sweep_stores(inputs, slopes, inputs_out, slopes_out, sems)
    forward_sweep(corrected[...], weights, biases, ref, inputs, slopes, stores)
    for store in sum(stores, []):
        store.wait()


def finish_block(scale, adjoint, transposed, inputs, slope, ref):
    channels = adjoint.shape[1]
    change = slope * adjoint
    adjoint = adjoint + convolve(ref, change, transposed)
    offset = jnp.sum(change, axis=0, keepdims=True) * scale
    moved = rows_from(ref, 1)
    field = jnp.concatenate([rows_from(inputs, row_at) for row_at in range(3)], axis=1)
    kernel = scale * lax.dot_general(
        field, moved, (((0,), (0,)), ((), ())), preferred_element_type=f32
    )
    taps = [
        kernel[
            row_at * channels : (row_at + 1) * channels,
            (2 - col_at) * channels : (3 - col_at) * channels,
        ]
        for row_at in range(3)
        for col_at in range(3)
    ]
    taps.append(jnp.broadcast_to(offset, (EXTRA, channels)))
    return adjoint, jnp.concatenate(taps, axis=0)


def final_body(scale, moving, transposed, inputs, slopes, adjoint_out, kernels_out, ref):
    clear_border(ref)
    adjoint = moving[...]
    for index in reversed(range(transposed.shape[0])):
        adjoint, kernels_out[index] = finish_block(
            scale, adjoint, transposed.at[index], inputs.at[index], slopes[index], ref
        )
    adjoint_out[...] = adjoint


def other_body(
    scale, first, last, moving, transposed, inputs, slopes, kernels, adjoint_out, kernels_out, ref
):
    clear_border(ref)
    adjoint = moving[...]
    for index in reversed(range(first, last)):
        adjoint, kernel = finish_block(
            scale, adjoint, transposed.at[index], inputs.at[index], slopes[index], ref
        )
        kernels_out[index - first] = kernels[index] + kernel
    if adjoint_out is not None:
        adjoint_out[...] = adjoint


def join_body(first, mine, theirs, late_offsets, kernels_out, offsets_out, total, sems):
    size = kernels_out.shape[1]
    count = mine.shape[0]
    part = size // 3
    copies = []
    for index in range(count):
        for at in range(3):
            rows = pl.ds(at * part, part)
            total[index, rows] = mine[index, rows] + theirs[index, rows]
            copy = pltpu.make_async_copy(
                total.at[index, rows], kernels_out.at[first + index, rows], sems.at[3 * index + at]
            )
            copy.start()
            copies.append(copy)
    offsets_out[:count] = mine[:, size] + theirs[:, size]
    if late_offsets is not None:
        offsets_out[count:] = late_offsets[...]
    for copy in copies:
        copy.wait()


def shards(images, weights, biases, end_grad):
    count, height, width, channels = images.shape
    blocks = weights.shape[0]
    rows = count * height * width
    part = rows // GROUP
    layers = lax.axis_size("layer")
    outer = layers // GROUP
    near = [[a * GROUP + b for b in range(GROUP)] for a in range(outer)]
    pair = [(i, i ^ GROUP) for i in range(layers)]
    around = [[(i, (i + 2 * GROUP * d) % layers) for i in range(layers)] for d in (1, 2, 3)]
    down = [[(i, i - 2 * GROUP * d) for i in range(2 * GROUP * d, layers)] for d in (1, 2, 3)]
    dp = lax.axis_size("dp")
    partner = [(i, (i + dp // 2) % dp) for i in range(dp)]
    sibling = [(i, i ^ 1) for i in range(dp)]
    spot = lax.axis_index("layer").astype(jnp.int32)
    spot = jnp.stack([spot >> 4, (spot >> 3) & 1])
    scale = 1.0 / (count * dp)
    per_conv = 2 * rows * 9 * channels * channels
    half = blocks // 2

    def exchange(value, groups):
        return lax.all_to_all(value, "layer", 0, 0, axis_index_groups=groups)

    plane = shape((rows, channels))
    kept = stored((rows, channels))
    matrix = shape((channels, channels))
    pieces_shape = shape((GROUP, part, channels))
    pieces_kept = stored((GROUP, part, channels))
    both_kept = stored((GROUP, part + channels, channels))
    both = shape((part + channels, channels))
    piece = shape((part, channels))
    matrices = stored((GROUP, channels, channels))
    taps_shape = shape((blocks, 9, channels, channels), bf16)
    sweep_shape = (blocks, 9 * channels, channels)
    inputs_dims = (blocks, count, height + 2, width, channels)
    slopes_dims = (blocks, rows, channels)
    offsets_shape = shape((blocks, channels))
    kernels_shape = shape((blocks, 9 * channels + EXTRA, channels))
    half_kernels = shape((half, 9 * channels + EXTRA, channels))
    result = jax.ShapeDtypeStruct((rows, channels), f32)
    gradients = jax.ShapeDtypeStruct((blocks, 9 * channels, channels), f32)
    half_offsets = jax.ShapeDtypeStruct((half, channels), f32)
    ref = pltpu.VMEM((count, height + 2, width, 3 * channels), bf16)
    dma = pltpu.SemaphoreType.DMA
    sweep_scratch = [pltpu.VMEM(inputs_dims, bf16), pltpu.VMEM(slopes_dims, f32)]

    flat = weights.reshape(blocks, 9, channels, channels)
    kernels = weights.reshape(sweep_shape)
    (own,) = call(
        coarse_body, [matrix], in_hbm(flat), ins=[HBM],
        scratch=[pltpu.VMEM((blocks, channels, channels), bf16), dma(())], name="coarse",
    )
    before = lax.ppermute(own, "layer", [(i, i + 1) for i in range(layers - 1)])
    after = lax.ppermute(own, "layer", [(i + 1, i) for i in range(layers - 1)])
    held, field, offsets, cotangent = call(
        load_body, [taps_shape, plane, offsets_shape, plane],
        in_hbm(flat), in_hbm(images.reshape(rows, channels)), in_hbm(biases),
        in_hbm(end_grad.reshape(rows, channels)),
        ins=[HBM] * 4, scratch=[dma((4,))], name="load",
    )

    (payload,) = call(
        start_body, [both_kept], field, own, before, held.reshape(sweep_shape), offsets,
        scratch=[ref], flops=blocks * per_conv, name="start",
    )
    first = exchange(payload, near)
    first, after = lax.optimization_barrier((first, after))
    starts, ends_adj, back = call(
        ends_body, [kept] * 3, field, cotangent, own, before, after, name="ends"
    )
    (transposed,) = call(flip_body, [stored(sweep_shape, bf16)], flat, name="flip")
    full, prefixes = call(total_body, [both, pieces_shape], first, name="total")
    their_full = lax.ppermute(full, "layer", pair)
    (pair_full,) = call(
        lambda *refs: pair_body(part, *refs), [both], spot, full, their_full,
        ins=[SMEM, VMEM, VMEM], name="pair",
    )
    around_full = [lax.ppermute(pair_full, "layer", to) for to in around]
    prefix, suffix = call(
        lambda *refs: products_body(part, *refs), [matrices] * 2, first, name="products"
    )
    replay_scratch = [pltpu.VMEM((GROUP, channels, channels), f32), dma(())]
    (error,) = call(
        replay_body, [pieces_kept], spot, their_full, *around_full, prefixes, in_hbm(prefix),
        ins=[SMEM] + [VMEM] * 5 + [HBM], scratch=replay_scratch, name="replay",
    )
    error, suffix, ends_adj, back, transposed, starts = lax.optimization_barrier(
        (error, suffix, ends_adj, back, transposed, starts)
    )
    error = exchange(error, near).reshape(rows, channels)

    corrected, interval_ends, inputs, slopes, adj_residual = call(
        middle_body, [kept, result, stored(inputs_dims, bf16), stored(slopes_dims), kept],
        error, in_hbm(starts), in_hbm(ends_adj), in_hbm(back), in_hbm(kernels),
        in_hbm(transposed), in_hbm(biases),
        ins=[VMEM] + [HBM] * 6, out_specs=[HBM, HBM, HBM, HBM, VMEM],
        scratch=[ref] + [pltpu.VMEM((rows, channels), f32)] * 2 + sweep_scratch
        + [pltpu.VMEM((rows, channels), f32)] * 3 + [pltpu.VMEM(sweep_shape, bf16)] * 2
        + [pltpu.VMEM((blocks, channels), f32), dma((2 * blocks + 2,)), dma((blocks + 5,))],
        flops=2 * blocks * per_conv, name="middle",
    )
    other_corrected = lax.ppermute(corrected, "dp", partner)
    pieces = exchange(adj_residual.reshape(GROUP, part, channels), near)
    total, prefixes = call(
        lambda *refs: back_total_body(part, *refs), [piece, pieces_kept], pieces, first,
        name="back_total",
    )
    total, other_corrected = lax.optimization_barrier((total, other_corrected))
    their_total = lax.ppermute(total, "layer", pair)
    (pair_total,) = call(
        lambda *refs: back_pair_body(part, *refs), [piece],
        spot, total, their_total, full, their_full, ins=[SMEM] + [VMEM] * 4, name="back_pair",
    )
    down_total = [lax.ppermute(pair_total, "layer", to) for to in down]
    other_inputs, other_slopes = call(
        again_body, [stored(inputs_dims, bf16), stored(slopes_dims)],
        other_corrected, kernels, offsets, out_specs=[HBM] * 2,
        scratch=[ref] + sweep_scratch + [dma((2 * blocks,))], flops=blocks * per_conv, name="again",
    )
    (adj_error,) = call(
        back_replay_body, [pieces_kept], spot, their_total, *down_total, their_full,
        around_full[2], around_full[1], prefixes, in_hbm(suffix),
        ins=[SMEM] + [VMEM] * 8 + [HBM], scratch=replay_scratch, name="back_replay",
    )
    adj_error, other_inputs, other_slopes = lax.optimization_barrier(
        (adj_error, other_inputs, other_slopes)
    )
    moving = ends_adj + exchange(adj_error, near).reshape(rows, channels)
    other_moving = lax.ppermute(moving, "dp", partner)
    adjoint, kernel_part = call(
        lambda *refs: final_body(scale, *refs), [result, kernels_shape],
        moving, transposed, inputs, slopes,
        scratch=[ref], flops=2 * blocks * per_conv, name="final",
    )
    other_moving, late = call(
        lambda *refs: other_body(scale, half, blocks, *refs), [plane, half_kernels],
        other_moving, transposed, other_inputs, other_slopes, kernel_part,
        scratch=[ref], flops=blocks * per_conv, name="other_late",
    )
    their_late = lax.ppermute(late, "dp", sibling)
    (early,) = call(
        lambda moving, a, b, c, d, out, ref: other_body(
            scale, 0, half, moving, a, b, c, d, None, out, ref
        ),
        [half_kernels], other_moving, transposed, other_inputs, other_slopes, kernel_part,
        scratch=[ref], flops=blocks * per_conv, name="other_early",
    )
    their_early = lax.ppermute(early, "dp", sibling)
    join_scratch = [pltpu.VMEM((half, 9 * channels, channels), f32), dma((3 * half,))]
    weight_grad, late_offsets = call(
        lambda mine, theirs, *refs: join_body(half, mine, theirs, None, *refs),
        [gradients, half_offsets], late, their_late,
        out_specs=[HBM, VMEM], scratch=join_scratch, name="join_late",
    )
    weight_grad, bias_grad = call(
        lambda mine, theirs, offsets, _, *refs: join_body(0, mine, theirs, offsets, *refs),
        [gradients, jax.ShapeDtypeStruct((blocks, channels), f32)],
        early, their_early, late_offsets, weight_grad,
        ins=[VMEM, VMEM, VMEM, HBM], out_specs=[HBM, VMEM], scratch=join_scratch,
        aliases={3: 0}, name="join_early",
    )
    dims = (1, count, height, width, channels)
    return (
        interval_ends.reshape(dims),
        adjoint.reshape(dims),
        weight_grad.reshape(blocks, 3, 3, channels, channels),
        bias_grad,
    )


def solution(mesh):
    in_specs = (
        P("dp", None, None, None),
        P("layer", None, None, None, None),
        P("layer", None),
        P("dp", None, None, None),
    )
    out_specs = (
        P("layer", "dp", None, None, None),
        P("layer", "dp", None, None, None),
        P("layer", None, None, None, None),
        P("layer", None),
    )
    return jax.shard_map(shards, mesh=mesh, in_specs=in_specs, out_specs=out_specs, check_vma=False)
```

```python
import math

import jax
import jax.numpy as jnp
from jax import lax
from jax.experimental import pallas as pl
from jax.experimental.pallas import tpu as pltpu
from jax.sharding import PartitionSpec as P

GROUP = 8
EXTRA = 8
VMEM_LIMIT = 12 * 1024 * 1024
f32 = jnp.float32
bf16 = jnp.bfloat16


def shifted_columns(value, width):
    rows = value.shape[0]
    at = lax.broadcasted_iota(jnp.int32, value.shape, 0) % width
    left = jnp.where(at == 0, 0.0, pltpu.roll(value, 1, 0))
    right = jnp.where(at == width - 1, 0.0, pltpu.roll(value, rows - 1, 0))
    return jnp.concatenate([left.astype(bf16), value.astype(bf16), right.astype(bf16)], axis=1)


def clear_border(ref):
    height = ref.shape[1]
    edge = jnp.zeros((ref.shape[0], 1) + ref.shape[2:], ref.dtype)
    ref[:, 0:1] = edge
    ref[:, height - 1 : height] = edge


def rows_from(ref, row_at):
    images, height, width, lanes = ref.shape
    return ref[:, row_at : row_at + height - 2].reshape(images * (height - 2) * width, lanes)


def convolve(ref, value, kernel):
    images, height, width, lanes = ref.shape
    rows = (height - 2) * width
    parts = []
    for image in range(images):
        moved = shifted_columns(value[image * rows : (image + 1) * rows], width)
        ref[image, 1 : height - 1] = moved.reshape(height - 2, width, lanes)
        window = [ref[image, at : at + height - 2].reshape(rows, lanes) for at in range(3)]
        parts.append(
            jnp.dot(jnp.concatenate(window, axis=1), kernel[...], preferred_element_type=f32)
        )
    return jnp.concatenate(parts, axis=0)


def split(value):
    high = value.astype(bf16)
    low = (value - high.astype(f32)).astype(bf16)
    return high, low


def times(value, matrix, transpose=False):
    dims = (((1,), (1 if transpose else 0,)), ((), ()))
    high, low = split(value)
    mhigh, mlow = split(matrix)
    dot = lambda a, b: lax.dot_general(a, b, dims, preferred_element_type=f32)
    return dot(high, mhigh) + (dot(low, mhigh) + dot(high, mlow))


VMEM = pl.BlockSpec(memory_space=pltpu.VMEM)
SMEM = pl.BlockSpec(memory_space=pltpu.SMEM)
HBM = pl.BlockSpec(memory_space=pltpu.HBM)


def call(body, outs, *args, ins=None, out_specs=None, scratch=(), flops=0, aliases=None, name=None):
    size = sum(a.size * a.dtype.itemsize for a in args)
    size += sum(math.prod(o.shape) * jnp.dtype(o.dtype).itemsize for o in outs)
    return pl.pallas_call(
        body,
        out_shape=tuple(outs),
        in_specs=list(ins) if ins else [VMEM] * len(args),
        out_specs=tuple(out_specs) if out_specs else (VMEM,) * len(outs),
        scratch_shapes=list(scratch),
        input_output_aliases=aliases or {},
        cost_estimate=pl.CostEstimate(flops=flops, bytes_accessed=size, transcendentals=0),
        compiler_params=pltpu.CompilerParams(vmem_limit_bytes=VMEM_LIMIT),
        name=name,
    )(*args)


def shape(dims, dtype=f32):
    return pltpu.VMEM(dims, dtype)


def stored(dims, dtype=f32):
    return pltpu.HBM(dims, dtype)


def in_hbm(value):
    return pltpu.with_memory_space_constraint(value, pltpu.HBM)


def coarse_body(weights, out, centre, sem):
    copy = pltpu.make_async_copy(weights.at[:, 4], centre, sem)
    copy.start()
    copy.wait()
    total = centre[0].astype(f32)
    for index in range(1, centre.shape[0]):
        total = total + centre[index].astype(f32)
    out[...] = 0.25 * total


def load_body(
    own, weights, images, biases, end_grad,
    copies_out, weights_out, images_out, biases_out, end_out, sems,
):
    pairs = [(weights, weights_out), (images, images_out), (biases, biases_out)]
    pairs.append((end_grad, end_out))
    copies = [pltpu.make_async_copy(a, b, sems.at[at]) for at, (a, b) in enumerate(pairs)]
    for copy in copies:
        copy.start()
    for index in range(GROUP):
        copies_out[index] = own[...]
    for copy in copies:
        copy.wait()


def flip_body(weights, transposed):
    taps, channels = weights.shape[1], weights.shape[2]
    for index in range(weights.shape[0]):
        for tap in range(taps):
            flipped = weights[index, taps - 1 - tap].astype(f32).T
            transposed[index, tap * channels : (tap + 1) * channels] = flipped.astype(bf16)


def start_body(images, own, before, weights, biases, residual, ref):
    clear_border(ref)
    field = images[...]
    state = field + times(field, before[...])
    for index in range(weights.shape[0]):
        state = state + 0.25 * jnp.tanh(
            convolve(ref, state, weights.at[index]) + biases[index : index + 1]
        )
    residual[...] = state - (field + times(field, own[...]))


def ends_body(images, end_grad, own, before, after, starts_out, ends_out, back_out):
    field = images[...]
    starts_out[...] = field + times(field, before[...])
    field = end_grad[...]
    ends_out[...] = field + times(field, after[...], True)
    back_out[...] = field + times(field, own[...], True)


def total_body(pieces, group, total, locals_out):
    error = pieces[0]
    for index in range(1, GROUP):
        locals_out[index] = error
        error = error + (times(error, group[index]) + pieces[index])
    total[...] = error


def pair_body(spot, mine, theirs, my_product, their_product, out):
    upper = spot[1] == 1
    early = jnp.where(upper, theirs[...], mine[...])
    late = jnp.where(upper, mine[...], theirs[...])
    product = jnp.where(upper, my_product[...], their_product[...])
    out[...] = early + (times(early, product) + late)


def pair_product_body(spot, mine, theirs, out):
    upper = spot[1] == 1
    early = jnp.where(upper, theirs[...], mine[...])
    late = jnp.where(upper, mine[...], theirs[...])
    out[...] = early + (times(early, late) + late)


def back_pair_body(spot, mine, theirs, my_product, their_product, out):
    upper = spot[1] == 1
    early = jnp.where(upper, mine[...], theirs[...])
    late = jnp.where(upper, theirs[...], mine[...])
    product = jnp.where(upper, their_product[...], my_product[...])
    out[...] = early + (times(early, product, True) + late)


def products_body(group, product_out, prefix_out, suffix_out):
    before = group[0]
    after = group[GROUP - 1]
    for index in range(1, GROUP):
        prefix_out[index] = before
        suffix_out[GROUP - 1 - index] = after
        matrix = group[index]
        before = before + (matrix + times(before, matrix))
        if index < GROUP - 1:
            matrix = group[GROUP - 1 - index]
            after = after + (matrix + times(matrix, after))
    product_out[...] = before


def back_total_body(pieces, group, total, locals_out):
    error = pieces[GROUP - 1]
    for index in range(GROUP - 2, -1, -1):
        locals_out[index] = error
        error = error + (times(error, group[index], True) + pieces[index])
    total[...] = error


def replay_body(
    spot, theirs, far1, far2, far3, their_product, product1, product2, locals_in, prefix_in,
    result, prefix, out, sem, sems,
):
    stores = [pltpu.make_async_copy(out.at[at], result.at[at], sems.at[at]) for at in range(GROUP)]
    copy = pltpu.make_async_copy(prefix_in, prefix, sem)
    copy.start()
    error = far3[...]
    for group, product in ((far2, product2), (far1, product1)):
        error = error + (times(error, product[...]) + group[...])
    longer = error + (times(error, their_product[...]) + theirs[...])
    error = jnp.where(spot[1] == 1, longer, error)
    out[0] = error
    stores[0].start()
    copy.wait()
    for index in range(1, GROUP):
        out[index] = error + (times(error, prefix[index]) + locals_in[index])
        stores[index].start()
    for store in stores:
        store.wait()


def back_replay_body(
    spot, theirs, far1, far2, far3, their_product, product1, product2, locals_in, suffix_in,
    result, suffix, out, sem, sems,
):
    stores = [pltpu.make_async_copy(out.at[at], result.at[at], sems.at[at]) for at in range(GROUP)]
    copy = pltpu.make_async_copy(suffix_in, suffix, sem)
    copy.start()
    error = far3[...]
    for group, product in ((far2, product2), (far1, product1)):
        error = error + (times(error, product[...], True) + group[...])
    longer = error + (times(error, their_product[...], True) + theirs[...])
    error = jnp.where(spot[1] == 0, longer, error)
    out[GROUP - 1] = error
    stores[GROUP - 1].start()
    copy.wait()
    for index in range(GROUP - 1):
        out[index] = error + (times(error, suffix[index], True) + locals_in[index])
        stores[index].start()
    for store in stores:
        store.wait()


def forward_sweep(state, weights, biases, ref, inputs, slopes, stores, fetches=None):
    for index in range(weights.shape[0]):
        if fetches is not None:
            fetches[index].wait()
        activation = jnp.tanh(convolve(ref, state, weights.at[index]) + biases[index : index + 1])
        channels = state.shape[1]
        inputs[index] = ref[:, :, :, channels : 2 * channels]
        slopes[index] = 0.25 * (1.0 - activation * activation)
        for store in stores[index]:
            store.start()
        state = state + 0.25 * activation
    return state


def sweep_stores(inputs, slopes, inputs_out, slopes_out, sems):
    blocks = inputs.shape[0]
    return [
        [
            pltpu.make_async_copy(inputs.at[index], inputs_out.at[index], sems.at[index]),
            pltpu.make_async_copy(slopes.at[index], slopes_out.at[index], sems.at[blocks + index]),
        ]
        for index in range(blocks)
    ]


def middle_body(
    corrected, ends_in, back_in, weights_in, transposed_in, biases_in,
    ends_out, inputs_out, slopes_out, residual_out,
    ref, ends, inputs, slopes, ends_adj, back, weights, transposed, biases, sems, loads,
):
    blocks = weights.shape[0]
    pairs = [(biases_in, biases)]
    pairs += [(weights_in.at[index], weights.at[index]) for index in range(blocks)]
    pairs += [(transposed_in, transposed), (ends_in, ends_adj), (back_in, back)]
    fetches = [pltpu.make_async_copy(a, b, loads.at[at]) for at, (a, b) in enumerate(pairs)]
    for fetch in fetches:
        fetch.start()
    clear_border(ref)
    stores = sweep_stores(inputs, slopes, inputs_out, slopes_out, sems)
    fetches[0].wait()
    ends[...] = forward_sweep(
        corrected[...], weights, biases, ref, inputs, slopes, stores, fetches[1 : 1 + blocks]
    )
    for fetch in fetches[1 + blocks :]:
        fetch.wait()
    last = pltpu.make_async_copy(ends, ends_out, sems.at[2 * blocks])
    last.start()
    adjoint = ends_adj[...]
    for index in reversed(range(blocks)):
        change = slopes[index] * adjoint
        adjoint = adjoint + convolve(ref, change, transposed.at[index])
    residual_out[...] = adjoint - back[...]
    for store in sum(stores, [last]):
        store.wait()


def again_body(corrected, weights, biases, inputs_out, slopes_out, ref, inputs, slopes, sems):
    clear_border(ref)
    stores = sweep_stores(inputs, slopes, inputs_out, slopes_out, sems)
    forward_sweep(corrected[...], weights, biases, ref, inputs, slopes, stores)
    for store in sum(stores, []):
        store.wait()


def finish_block(scale, adjoint, transposed, inputs, slope, ref):
    channels = adjoint.shape[1]
    change = slope * adjoint
    adjoint = adjoint + convolve(ref, change, transposed)
    offset = jnp.sum(change, axis=0, keepdims=True) * scale
    moved = rows_from(ref, 1)
    field = jnp.concatenate([rows_from(inputs, row_at) for row_at in range(3)], axis=1)
    kernel = scale * lax.dot_general(
        field, moved, (((0,), (0,)), ((), ())), preferred_element_type=f32
    )
    taps = [
        kernel[
            row_at * channels : (row_at + 1) * channels,
            (2 - col_at) * channels : (3 - col_at) * channels,
        ]
        for row_at in range(3)
        for col_at in range(3)
    ]
    taps.append(jnp.broadcast_to(offset, (EXTRA, channels)))
    return adjoint, jnp.concatenate(taps, axis=0)


def final_body(scale, moving, transposed, inputs, slopes, adjoint_out, kernels_out, ref):
    clear_border(ref)
    adjoint = moving[...]
    for index in reversed(range(transposed.shape[0])):
        adjoint, kernels_out[index] = finish_block(
            scale, adjoint, transposed.at[index], inputs.at[index], slopes[index], ref
        )
    adjoint_out[...] = adjoint


def other_body(
    scale, first, last, moving, transposed, inputs, slopes, kernels, adjoint_out, kernels_out, ref
):
    clear_border(ref)
    adjoint = moving[...]
    for index in reversed(range(first, last)):
        adjoint, kernel = finish_block(
            scale, adjoint, transposed.at[index], inputs.at[index], slopes[index], ref
        )
        kernels_out[index - first] = kernels[index] + kernel
    if adjoint_out is not None:
        adjoint_out[...] = adjoint


def join_body(first, mine, theirs, late, kernels_out, offsets_out, total, offsets, sems):
    size = kernels_out.shape[1]
    count = mine.shape[0]
    offsets[:count] = mine[:, size] + theirs[:, size]
    if late is not None:
        offsets[count:] = late[...]
    copies = [pltpu.make_async_copy(offsets, offsets_out, sems.at[count])]
    copies[0].start()
    for index in range(count):
        total[index] = mine[index, :size] + theirs[index, :size]
        copies.append(
            pltpu.make_async_copy(total.at[index], kernels_out.at[first + index], sems.at[index])
        )
        copies[-1].start()
    for copy in copies:
        copy.wait()


def shards(images, weights, biases, end_grad):
    count, height, width, channels = images.shape
    blocks = weights.shape[0]
    rows = count * height * width
    part = rows // GROUP
    layers = lax.axis_size("layer")
    outer = layers // GROUP
    near = [[a * GROUP + b for b in range(GROUP)] for a in range(outer)]
    pair = [(i, i ^ GROUP) for i in range(layers)]
    around = [[(i, (i + 2 * GROUP * d) % layers) for i in range(layers)] for d in (1, 2, 3)]
    up = [[(i, i + 2 * GROUP * d) for i in range(layers - 2 * GROUP * d)] for d in (1, 2, 3)]
    down = [[(i, i - 2 * GROUP * d) for i in range(2 * GROUP * d, layers)] for d in (1, 2, 3)]
    dp = lax.axis_size("dp")
    partner = [(i, (i + dp // 2) % dp) for i in range(dp)]
    sibling = [(i, i ^ 1) for i in range(dp)]
    spot = lax.axis_index("layer").astype(jnp.int32)
    spot = jnp.stack([spot >> 4, (spot >> 3) & 1])
    scale = 1.0 / (count * dp)
    per_conv = 2 * rows * 9 * channels * channels
    half = blocks // 2

    def exchange(value, groups):
        return lax.all_to_all(value, "layer", 0, 0, axis_index_groups=groups)

    plane = shape((rows, channels))
    kept = stored((rows, channels))
    matrix = shape((channels, channels))
    pieces_shape = shape((GROUP, part, channels))
    pieces_kept = stored((GROUP, part, channels))
    piece = shape((part, channels))
    matrices = stored((GROUP, channels, channels))
    taps_shape = shape((blocks, 9, channels, channels), bf16)
    sweep_shape = (blocks, 9 * channels, channels)
    inputs_dims = (blocks, count, height + 2, width, channels)
    slopes_dims = (blocks, rows, channels)
    offsets_shape = shape((blocks, channels))
    kernels_shape = shape((blocks, 9 * channels + EXTRA, channels))
    half_kernels = shape((half, 9 * channels + EXTRA, channels))
    result = jax.ShapeDtypeStruct((rows, channels), f32)
    gradients = jax.ShapeDtypeStruct((blocks, 9 * channels, channels), f32)
    half_offsets = jax.ShapeDtypeStruct((half, channels), f32)
    ref = pltpu.VMEM((count, height + 2, width, 3 * channels), bf16)
    dma = pltpu.SemaphoreType.DMA
    sweep_scratch = [pltpu.VMEM(inputs_dims, bf16), pltpu.VMEM(slopes_dims, f32)]

    flat = weights.reshape(blocks, 9, channels, channels)
    kernels = weights.reshape(sweep_shape)
    (own,) = call(
        coarse_body, [matrix], in_hbm(flat), ins=[HBM],
        scratch=[pltpu.VMEM((blocks, channels, channels), bf16), dma(())], name="coarse",
    )
    before = lax.ppermute(own, "layer", [(i, i + 1) for i in range(layers - 1)])
    after = lax.ppermute(own, "layer", [(i + 1, i) for i in range(layers - 1)])
    copies, held, field, offsets, cotangent = call(
        load_body, [matrices, taps_shape, plane, offsets_shape, plane], own,
        in_hbm(flat), in_hbm(images.reshape(rows, channels)), in_hbm(biases),
        in_hbm(end_grad.reshape(rows, channels)),
        ins=[VMEM] + [HBM] * 4, scratch=[dma((4,))], name="load",
    )
    group = exchange(copies, near)

    (residual,) = call(
        start_body, [kept], field, own, before, held.reshape(sweep_shape), offsets,
        scratch=[ref], flops=blocks * per_conv, name="start",
    )
    residual, group = lax.optimization_barrier((residual, group))
    first = exchange(residual.reshape(GROUP, part, channels), near)
    product, prefix, suffix = call(
        products_body, [matrix, matrices, matrices], group, name="products"
    )
    their_product = lax.ppermute(product, "layer", pair)
    (pair_product,) = call(
        pair_product_body, [matrix], spot, product, their_product, ins=[SMEM, VMEM, VMEM],
        name="pair_product",
    )
    around_product = [lax.ppermute(pair_product, "layer", to) for to in around]
    starts, ends_adj, back = call(
        ends_body, [kept] * 3, field, cotangent, own, before, after, name="ends"
    )
    (transposed,) = call(flip_body, [stored(sweep_shape, bf16)], flat, name="flip")
    first, starts, ends_adj, back, transposed = lax.optimization_barrier(
        (first, starts, ends_adj, back, transposed)
    )
    total, prefixes = call(total_body, [piece, pieces_shape], first, group, name="total")
    their_total = lax.ppermute(total, "layer", pair)
    (pair_total,) = call(
        pair_body, [piece], spot, total, their_total, product, their_product,
        ins=[SMEM] + [VMEM] * 4, name="pair",
    )
    up_total = [lax.ppermute(pair_total, "layer", to) for to in up]
    replay_scratch = [
        pltpu.VMEM((GROUP, channels, channels), f32), pltpu.VMEM((GROUP, part, channels), f32),
        dma(()), dma((GROUP,)),
    ]
    (error,) = call(
        replay_body, [pieces_kept], spot, their_total, *up_total, their_product,
        around_product[0], around_product[1], prefixes, in_hbm(prefix),
        ins=[SMEM] + [VMEM] * 8 + [HBM], out_specs=[HBM], scratch=replay_scratch, name="replay",
    )
    error, suffix = lax.optimization_barrier((error, suffix))
    corrected = starts + exchange(error, near).reshape(rows, channels)
    other_corrected = lax.ppermute(corrected, "dp", partner)

    interval_ends, inputs, slopes, adj_residual = call(
        middle_body, [result, stored(inputs_dims, bf16), stored(slopes_dims), kept],
        corrected, in_hbm(ends_adj), in_hbm(back), in_hbm(kernels),
        in_hbm(transposed), in_hbm(biases),
        ins=[VMEM] + [HBM] * 5, out_specs=[HBM, HBM, HBM, VMEM],
        scratch=[ref, pltpu.VMEM((rows, channels), f32)] + sweep_scratch
        + [pltpu.VMEM((rows, channels), f32)] * 2 + [pltpu.VMEM(sweep_shape, bf16)] * 2
        + [pltpu.VMEM((blocks, channels), f32), dma((2 * blocks + 1,)), dma((blocks + 4,))],
        flops=2 * blocks * per_conv, name="middle",
    )
    pieces = exchange(adj_residual.reshape(GROUP, part, channels), near)
    total, prefixes = call(
        back_total_body, [piece, pieces_kept], pieces, group,
        name="back_total",
    )
    their_total = lax.ppermute(total, "layer", pair)
    (pair_total,) = call(
        back_pair_body, [piece], spot, total, their_total, product, their_product,
        ins=[SMEM] + [VMEM] * 4, name="back_pair",
    )
    down_total = [lax.ppermute(pair_total, "layer", to) for to in down]
    other_inputs, other_slopes = call(
        again_body, [stored(inputs_dims, bf16), stored(slopes_dims)],
        other_corrected, kernels, offsets, out_specs=[HBM] * 2,
        scratch=[ref] + sweep_scratch + [dma((2 * blocks,))], flops=blocks * per_conv, name="again",
    )
    (adj_error,) = call(
        back_replay_body, [pieces_kept], spot, their_total, *down_total, their_product,
        around_product[2], around_product[1], prefixes, in_hbm(suffix),
        ins=[SMEM] + [VMEM] * 8 + [HBM], out_specs=[HBM], scratch=replay_scratch,
        name="back_replay",
    )
    adj_error, other_inputs, other_slopes = lax.optimization_barrier(
        (adj_error, other_inputs, other_slopes)
    )
    moving = ends_adj + exchange(adj_error, near).reshape(rows, channels)
    other_moving = lax.ppermute(moving, "dp", partner)
    adjoint, kernel_part = call(
        lambda *refs: final_body(scale, *refs), [result, kernels_shape],
        moving, transposed, inputs, slopes,
        scratch=[ref], flops=2 * blocks * per_conv, name="final",
    )
    other_moving, late = call(
        lambda *refs: other_body(scale, half, blocks, *refs), [plane, half_kernels],
        other_moving, transposed, other_inputs, other_slopes, kernel_part,
        scratch=[ref], flops=blocks * per_conv, name="other_late",
    )
    their_late = lax.ppermute(late, "dp", sibling)
    (early,) = call(
        lambda moving, a, b, c, d, out, ref: other_body(
            scale, 0, half, moving, a, b, c, d, None, out, ref
        ),
        [half_kernels], other_moving, transposed, other_inputs, other_slopes, kernel_part,
        scratch=[ref], flops=blocks * per_conv, name="other_early",
    )
    their_early = lax.ppermute(early, "dp", sibling)
    sums = pltpu.VMEM((half, 9 * channels, channels), f32)
    weight_grad, late_offsets = call(
        lambda mine, theirs, *refs: join_body(half, mine, theirs, None, *refs),
        [gradients, half_offsets], late, their_late,
        out_specs=[HBM, HBM], name="join_late",
        scratch=[sums, pltpu.VMEM((half, channels), f32), dma((half + 1,))],
    )
    weight_grad, bias_grad = call(
        lambda mine, theirs, offsets, _, *refs: join_body(0, mine, theirs, offsets, *refs),
        [gradients, jax.ShapeDtypeStruct((blocks, channels), f32)],
        early, their_early, late_offsets, weight_grad,
        ins=[VMEM, VMEM, VMEM, HBM], out_specs=[HBM, HBM], aliases={3: 0}, name="join_early",
        scratch=[sums, pltpu.VMEM((blocks, channels), f32), dma((half + 1,))],
    )
    dims = (1, count, height, width, channels)
    return (
        interval_ends.reshape(dims),
        adjoint.reshape(dims),
        weight_grad.reshape(blocks, 3, 3, channels, channels),
        bias_grad,
    )


def solution(mesh):
    in_specs = (
        P("dp", None, None, None),
        P("layer", None, None, None, None),
        P("layer", None),
        P("dp", None, None, None),
    )
    out_specs = (
        P("layer", "dp", None, None, None),
        P("layer", "dp", None, None, None),
        P("layer", None, None, None, None),
        P("layer", None),
    )
    return jax.shard_map(shards, mesh=mesh, in_specs=in_specs, out_specs=out_specs, check_vma=False)
```

```python
import math

import jax
import jax.numpy as jnp
from jax import lax
from jax.experimental import pallas as pl
from jax.experimental.pallas import tpu as pltpu
from jax.sharding import PartitionSpec as P

GROUP = 8
EXTRA = 8
VMEM_LIMIT = 12 * 1024 * 1024
f32 = jnp.float32
bf16 = jnp.bfloat16


def shifted_columns(value, width):
    rows = value.shape[0]
    at = lax.broadcasted_iota(jnp.int32, value.shape, 0) % width
    left = jnp.where(at == 0, 0.0, pltpu.roll(value, 1, 0))
    right = jnp.where(at == width - 1, 0.0, pltpu.roll(value, rows - 1, 0))
    return jnp.concatenate([left.astype(bf16), value.astype(bf16), right.astype(bf16)], axis=1)


def clear_border(ref):
    height = ref.shape[1]
    edge = jnp.zeros((ref.shape[0], 1) + ref.shape[2:], ref.dtype)
    ref[:, 0:1] = edge
    ref[:, height - 1 : height] = edge


def rows_from(ref, row_at):
    images, height, width, lanes = ref.shape
    return ref[:, row_at : row_at + height - 2].reshape(images * (height - 2) * width, lanes)


def convolve(ref, value, kernel):
    images, height, width, lanes = ref.shape
    rows = (height - 2) * width
    parts = []
    for image in range(images):
        moved = shifted_columns(value[image * rows : (image + 1) * rows], width)
        ref[image, 1 : height - 1] = moved.reshape(height - 2, width, lanes)
        window = [ref[image, at : at + height - 2].reshape(rows, lanes) for at in range(3)]
        parts.append(
            jnp.dot(jnp.concatenate(window, axis=1), kernel[...], preferred_element_type=f32)
        )
    return jnp.concatenate(parts, axis=0)


def split(value):
    high = value.astype(bf16)
    low = (value - high.astype(f32)).astype(bf16)
    return high, low


def times(value, matrix, transpose=False):
    dims = (((1,), (1 if transpose else 0,)), ((), ()))
    high, low = split(value)
    mhigh, mlow = split(matrix)
    dot = lambda a, b: lax.dot_general(a, b, dims, preferred_element_type=f32)
    return dot(high, mhigh) + (dot(low, mhigh) + dot(high, mlow))


VMEM = pl.BlockSpec(memory_space=pltpu.VMEM)
SMEM = pl.BlockSpec(memory_space=pltpu.SMEM)
HBM = pl.BlockSpec(memory_space=pltpu.HBM)


def call(body, outs, *args, ins=None, out_specs=None, scratch=(), flops=0, aliases=None, name=None):
    size = sum(a.size * a.dtype.itemsize for a in args)
    size += sum(math.prod(o.shape) * jnp.dtype(o.dtype).itemsize for o in outs)
    return pl.pallas_call(
        body,
        out_shape=tuple(outs),
        in_specs=list(ins) if ins else [VMEM] * len(args),
        out_specs=tuple(out_specs) if out_specs else (VMEM,) * len(outs),
        scratch_shapes=list(scratch),
        input_output_aliases=aliases or {},
        cost_estimate=pl.CostEstimate(flops=flops, bytes_accessed=size, transcendentals=0),
        compiler_params=pltpu.CompilerParams(vmem_limit_bytes=VMEM_LIMIT),
        name=name,
    )(*args)


def shape(dims, dtype=f32):
    return pltpu.VMEM(dims, dtype)


def stored(dims, dtype=f32):
    return pltpu.HBM(dims, dtype)


def in_hbm(value):
    return pltpu.with_memory_space_constraint(value, pltpu.HBM)


def coarse_body(weights, out, centre, sem):
    copy = pltpu.make_async_copy(weights.at[:, 4], centre, sem)
    copy.start()
    copy.wait()
    total = centre[0].astype(f32)
    for index in range(1, centre.shape[0]):
        total = total + centre[index].astype(f32)
    out[...] = 0.25 * total


def load_body(
    weights, images, biases, end_grad, weights_out, images_out, biases_out, end_out, sems
):
    pairs = [(weights, weights_out), (images, images_out), (biases, biases_out)]
    pairs.append((end_grad, end_out))
    copies = [pltpu.make_async_copy(a, b, sems.at[at]) for at, (a, b) in enumerate(pairs)]
    for copy in copies:
        copy.start()
    for copy in copies:
        copy.wait()


def flip_body(weights, transposed):
    taps, channels = weights.shape[1], weights.shape[2]
    for index in range(weights.shape[0]):
        for tap in range(taps):
            flipped = weights[index, taps - 1 - tap].astype(f32).T
            transposed[index, tap * channels : (tap + 1) * channels] = flipped.astype(bf16)


def start_body(images, own, before, weights, biases, payload, ref):
    clear_border(ref)
    field = images[...]
    state = field + times(field, before[...])
    for index in range(weights.shape[0]):
        state = state + 0.25 * jnp.tanh(
            convolve(ref, state, weights.at[index]) + biases[index : index + 1]
        )
    matrix = own[...]
    residual = state - (field + times(field, matrix))
    part = residual.shape[0] // GROUP
    for index in range(GROUP):
        payload[index, :part] = residual[index * part : (index + 1) * part]
        payload[index, part:] = matrix


def ends_body(images, end_grad, own, before, after, starts_out, ends_out, back_out):
    field = images[...]
    starts_out[...] = field + times(field, before[...])
    field = end_grad[...]
    ends_out[...] = field + times(field, after[...], True)
    back_out[...] = field + times(field, own[...], True)


def total_body(pieces, payload, locals_out):
    part = locals_out.shape[1]
    error = pieces[0, :part]
    product = pieces[0, part:]
    for index in range(1, GROUP):
        matrix = pieces[index, part:]
        locals_out[index] = error
        error = error + (times(error, matrix) + pieces[index, :part])
        product = product + (matrix + times(product, matrix))
    payload[:part] = error
    payload[part:] = product


def pair_body(part, spot, mine, theirs, out):
    upper = spot[1] == 1
    early = jnp.where(upper, theirs[...], mine[...])
    late = jnp.where(upper, mine[...], theirs[...])
    out[...] = early + (times(early, late[part:]) + late)


def back_pair_body(part, spot, mine, theirs, mine_full, theirs_full, out):
    upper = spot[1] == 1
    early = jnp.where(upper, mine[...], theirs[...])
    late = jnp.where(upper, theirs[...], mine[...])
    matrix = jnp.where(upper, theirs_full[part:], mine_full[part:])
    out[...] = early + (times(early, matrix, True) + late)


def products_body(part, pieces, prefix_out, suffix_out):
    before = pieces[0, part:]
    after = pieces[GROUP - 1, part:]
    for index in range(1, GROUP):
        prefix_out[index] = before
        suffix_out[GROUP - 1 - index] = after
        if index < GROUP - 1:
            matrix = pieces[index, part:]
            before = before + (matrix + times(before, matrix))
            matrix = pieces[GROUP - 1 - index, part:]
            after = after + (matrix + times(matrix, after))


def back_total_body(part, pieces, first, payload, locals_out):
    error = pieces[GROUP - 1]
    for index in range(GROUP - 2, -1, -1):
        locals_out[index] = error
        error = error + (times(error, first[index, part:], True) + pieces[index])
    payload[...] = error


def replay_body(
    spot, theirs, far1, far2, far3, locals_in, prefix_in, result, prefix, out, sem, sems
):
    stores = [pltpu.make_async_copy(out.at[at], result.at[at], sems.at[at]) for at in range(GROUP)]
    copy = pltpu.make_async_copy(prefix_in, prefix, sem)
    copy.start()
    part = out.shape[1]
    error = jnp.where(spot[0] >= 3, far3[:part], 0.0)
    for distance, group in ((2, far2), (1, far1)):
        longer = error + (times(error, group[part:]) + group[:part])
        error = jnp.where(spot[0] >= distance, longer, error)
    longer = error + (times(error, theirs[part:]) + theirs[:part])
    error = jnp.where(spot[1] == 1, longer, error)
    out[0] = error
    stores[0].start()
    copy.wait()
    for index in range(1, GROUP):
        out[index] = error + (times(error, prefix[index]) + locals_in[index])
        stores[index].start()
    for store in stores:
        store.wait()


def back_replay_body(
    spot, theirs, far1, far2, far3, theirs_full, full1, full2, locals_in, suffix_in,
    result, suffix, out, sem, sems,
):
    stores = [pltpu.make_async_copy(out.at[at], result.at[at], sems.at[at]) for at in range(GROUP)]
    copy = pltpu.make_async_copy(suffix_in, suffix, sem)
    copy.start()
    part = out.shape[1]
    error = far3[...]
    for group, full in ((far2, full2), (far1, full1)):
        error = error + (times(error, full[part:], True) + group[...])
    longer = error + (times(error, theirs_full[part:], True) + theirs[...])
    error = jnp.where(spot[1] == 0, longer, error)
    out[GROUP - 1] = error
    stores[GROUP - 1].start()
    copy.wait()
    for index in range(GROUP - 1):
        out[index] = error + (times(error, suffix[index], True) + locals_in[index])
        stores[index].start()
    for store in stores:
        store.wait()


def forward_sweep(state, weights, biases, ref, inputs, slopes, stores, fetches=None):
    for index in range(weights.shape[0]):
        if fetches is not None:
            fetches[index].wait()
        activation = jnp.tanh(convolve(ref, state, weights.at[index]) + biases[index : index + 1])
        channels = state.shape[1]
        inputs[index] = ref[:, :, :, channels : 2 * channels]
        slopes[index] = 0.25 * (1.0 - activation * activation)
        for store in stores[index]:
            store.start()
        state = state + 0.25 * activation
    return state


def sweep_stores(inputs, slopes, inputs_out, slopes_out, sems):
    blocks = inputs.shape[0]
    return [
        [
            pltpu.make_async_copy(inputs.at[index], inputs_out.at[index], sems.at[index]),
            pltpu.make_async_copy(slopes.at[index], slopes_out.at[index], sems.at[blocks + index]),
        ]
        for index in range(blocks)
    ]


def middle_body(
    corrected, ends_in, back_in, weights_in, transposed_in, biases_in,
    ends_out, inputs_out, slopes_out, residual_out,
    ref, ends, inputs, slopes, ends_adj, back, weights, transposed, biases, sems, loads,
):
    blocks = weights.shape[0]
    pairs = [(biases_in, biases)]
    pairs += [(weights_in.at[index], weights.at[index]) for index in range(blocks)]
    pairs += [(transposed_in, transposed), (ends_in, ends_adj), (back_in, back)]
    fetches = [pltpu.make_async_copy(a, b, loads.at[at]) for at, (a, b) in enumerate(pairs)]
    for fetch in fetches:
        fetch.start()
    clear_border(ref)
    stores = sweep_stores(inputs, slopes, inputs_out, slopes_out, sems)
    fetches[0].wait()
    ends[...] = forward_sweep(
        corrected[...], weights, biases, ref, inputs, slopes, stores, fetches[1 : 1 + blocks]
    )
    for fetch in fetches[1 + blocks :]:
        fetch.wait()
    last = pltpu.make_async_copy(ends, ends_out, sems.at[2 * blocks])
    last.start()
    adjoint = ends_adj[...]
    for index in reversed(range(blocks)):
        change = slopes[index] * adjoint
        adjoint = adjoint + convolve(ref, change, transposed.at[index])
    residual_out[...] = adjoint - back[...]
    for store in sum(stores, [last]):
        store.wait()


def again_body(corrected, weights, biases, inputs_out, slopes_out, ref, inputs, slopes, sems):
    clear_border(ref)
    stores = sweep_stores(inputs, slopes, inputs_out, slopes_out, sems)
    forward_sweep(corrected[...], weights, biases, ref, inputs, slopes, stores)
    for store in sum(stores, []):
        store.wait()


def finish_block(scale, adjoint, transposed, inputs, slope, ref):
    channels = adjoint.shape[1]
    change = slope * adjoint
    adjoint = adjoint + convolve(ref, change, transposed)
    offset = jnp.sum(change, axis=0, keepdims=True) * scale
    moved = rows_from(ref, 1)
    field = jnp.concatenate([rows_from(inputs, row_at) for row_at in range(3)], axis=1)
    kernel = scale * lax.dot_general(
        field, moved, (((0,), (0,)), ((), ())), preferred_element_type=f32
    )
    taps = [
        kernel[
            row_at * channels : (row_at + 1) * channels,
            (2 - col_at) * channels : (3 - col_at) * channels,
        ]
        for row_at in range(3)
        for col_at in range(3)
    ]
    taps.append(jnp.broadcast_to(offset, (EXTRA, channels)))
    return adjoint, jnp.concatenate(taps, axis=0)


def final_body(scale, moving, transposed, inputs, slopes, adjoint_out, kernels_out, ref):
    clear_border(ref)
    adjoint = moving[...]
    for index in reversed(range(transposed.shape[0])):
        adjoint, kernels_out[index] = finish_block(
            scale, adjoint, transposed.at[index], inputs.at[index], slopes[index], ref
        )
    adjoint_out[...] = adjoint


def other_body(
    scale, first, last, moving, transposed, inputs, slopes, kernels, adjoint_out, kernels_out, ref
):
    clear_border(ref)
    adjoint = moving[...]
    for index in reversed(range(first, last)):
        adjoint, kernel = finish_block(
            scale, adjoint, transposed.at[index], inputs.at[index], slopes[index], ref
        )
        kernels_out[index - first] = kernels[index] + kernel
    if adjoint_out is not None:
        adjoint_out[...] = adjoint


def join_body(first, mine, theirs, late, kernels_out, offsets_out, total, offsets, sems):
    size = kernels_out.shape[1]
    count = mine.shape[0]
    offsets[:count] = mine[:, size] + theirs[:, size]
    if late is not None:
        offsets[count:] = late[...]
    copies = [pltpu.make_async_copy(offsets, offsets_out, sems.at[count])]
    copies[0].start()
    for index in range(count):
        total[index] = mine[index, :size] + theirs[index, :size]
        copies.append(
            pltpu.make_async_copy(total.at[index], kernels_out.at[first + index], sems.at[index])
        )
        copies[-1].start()
    for copy in copies:
        copy.wait()


def shards(images, weights, biases, end_grad):
    count, height, width, channels = images.shape
    blocks = weights.shape[0]
    rows = count * height * width
    part = rows // GROUP
    layers = lax.axis_size("layer")
    outer = layers // GROUP
    near = [[a * GROUP + b for b in range(GROUP)] for a in range(outer)]
    pair = [(i, i ^ GROUP) for i in range(layers)]
    around = [[(i, (i + 2 * GROUP * d) % layers) for i in range(layers)] for d in (1, 2, 3)]
    down = [[(i, i - 2 * GROUP * d) for i in range(2 * GROUP * d, layers)] for d in (1, 2, 3)]
    dp = lax.axis_size("dp")
    partner = [(i, (i + dp // 2) % dp) for i in range(dp)]
    sibling = [(i, i ^ 1) for i in range(dp)]
    spot = lax.axis_index("layer").astype(jnp.int32)
    spot = jnp.stack([spot >> 4, (spot >> 3) & 1])
    scale = 1.0 / (count * dp)
    per_conv = 2 * rows * 9 * channels * channels
    half = blocks // 2

    def exchange(value, groups):
        return lax.all_to_all(value, "layer", 0, 0, axis_index_groups=groups)

    plane = shape((rows, channels))
    kept = stored((rows, channels))
    matrix = shape((channels, channels))
    pieces_shape = shape((GROUP, part, channels))
    pieces_kept = stored((GROUP, part, channels))
    both_kept = stored((GROUP, part + channels, channels))
    both = shape((part + channels, channels))
    piece = shape((part, channels))
    matrices = stored((GROUP, channels, channels))
    taps_shape = shape((blocks, 9, channels, channels), bf16)
    sweep_shape = (blocks, 9 * channels, channels)
    inputs_dims = (blocks, count, height + 2, width, channels)
    slopes_dims = (blocks, rows, channels)
    offsets_shape = shape((blocks, channels))
    kernels_shape = shape((blocks, 9 * channels + EXTRA, channels))
    half_kernels = shape((half, 9 * channels + EXTRA, channels))
    result = jax.ShapeDtypeStruct((rows, channels), f32)
    gradients = jax.ShapeDtypeStruct((blocks, 9 * channels, channels), f32)
    half_offsets = jax.ShapeDtypeStruct((half, channels), f32)
    ref = pltpu.VMEM((count, height + 2, width, 3 * channels), bf16)
    dma = pltpu.SemaphoreType.DMA
    sweep_scratch = [pltpu.VMEM(inputs_dims, bf16), pltpu.VMEM(slopes_dims, f32)]

    flat = weights.reshape(blocks, 9, channels, channels)
    kernels = weights.reshape(sweep_shape)
    (own,) = call(
        coarse_body, [matrix], in_hbm(flat), ins=[HBM],
        scratch=[pltpu.VMEM((blocks, channels, channels), bf16), dma(())], name="coarse",
    )
    before = lax.ppermute(own, "layer", [(i, i + 1) for i in range(layers - 1)])
    after = lax.ppermute(own, "layer", [(i + 1, i) for i in range(layers - 1)])
    held, field, offsets, cotangent = call(
        load_body, [taps_shape, plane, offsets_shape, plane],
        in_hbm(flat), in_hbm(images.reshape(rows, channels)), in_hbm(biases),
        in_hbm(end_grad.reshape(rows, channels)),
        ins=[HBM] * 4, scratch=[dma((4,))], name="load",
    )

    (payload,) = call(
        start_body, [both_kept], field, own, before, held.reshape(sweep_shape), offsets,
        scratch=[ref], flops=blocks * per_conv, name="start",
    )
    first = exchange(payload, near)
    starts, ends_adj, back = call(
        ends_body, [kept] * 3, field, cotangent, own, before, after, name="ends"
    )
    (transposed,) = call(flip_body, [stored(sweep_shape, bf16)], flat, name="flip")
    first, starts, ends_adj, back, transposed = lax.optimization_barrier(
        (first, starts, ends_adj, back, transposed)
    )
    full, prefixes = call(total_body, [both, pieces_shape], first, name="total")
    their_full = lax.ppermute(full, "layer", pair)
    (pair_full,) = call(
        lambda *refs: pair_body(part, *refs), [both], spot, full, their_full,
        ins=[SMEM, VMEM, VMEM], name="pair",
    )
    around_full = [lax.ppermute(pair_full, "layer", to) for to in around]
    prefix, suffix = call(
        lambda *refs: products_body(part, *refs), [matrices] * 2, first, name="products"
    )
    replay_scratch = [
        pltpu.VMEM((GROUP, channels, channels), f32), pltpu.VMEM((GROUP, part, channels), f32),
        dma(()), dma((GROUP,)),
    ]
    (error,) = call(
        replay_body, [pieces_kept], spot, their_full, *around_full, prefixes, in_hbm(prefix),
        ins=[SMEM] + [VMEM] * 5 + [HBM], out_specs=[HBM], scratch=replay_scratch, name="replay",
    )
    error, suffix = lax.optimization_barrier((error, suffix))
    corrected = starts + exchange(error, near).reshape(rows, channels)
    other_corrected = lax.ppermute(corrected, "dp", partner)

    interval_ends, inputs, slopes, adj_residual = call(
        middle_body, [result, stored(inputs_dims, bf16), stored(slopes_dims), kept],
        corrected, in_hbm(ends_adj), in_hbm(back), in_hbm(kernels),
        in_hbm(transposed), in_hbm(biases),
        ins=[VMEM] + [HBM] * 5, out_specs=[HBM, HBM, HBM, VMEM],
        scratch=[ref, pltpu.VMEM((rows, channels), f32)] + sweep_scratch
        + [pltpu.VMEM((rows, channels), f32)] * 2 + [pltpu.VMEM(sweep_shape, bf16)] * 2
        + [pltpu.VMEM((blocks, channels), f32), dma((2 * blocks + 1,)), dma((blocks + 4,))],
        flops=2 * blocks * per_conv, name="middle",
    )
    pieces = exchange(adj_residual.reshape(GROUP, part, channels), near)
    total, prefixes = call(
        lambda *refs: back_total_body(part, *refs), [piece, pieces_kept], pieces, first,
        name="back_total",
    )
    their_total = lax.ppermute(total, "layer", pair)
    (pair_total,) = call(
        lambda *refs: back_pair_body(part, *refs), [piece],
        spot, total, their_total, full, their_full, ins=[SMEM] + [VMEM] * 4, name="back_pair",
    )
    down_total = [lax.ppermute(pair_total, "layer", to) for to in down]
    other_inputs, other_slopes = call(
        again_body, [stored(inputs_dims, bf16), stored(slopes_dims)],
        other_corrected, kernels, offsets, out_specs=[HBM] * 2,
        scratch=[ref] + sweep_scratch + [dma((2 * blocks,))], flops=blocks * per_conv, name="again",
    )
    (adj_error,) = call(
        back_replay_body, [pieces_kept], spot, their_total, *down_total, their_full,
        around_full[2], around_full[1], prefixes, in_hbm(suffix),
        ins=[SMEM] + [VMEM] * 8 + [HBM], out_specs=[HBM], scratch=replay_scratch,
        name="back_replay",
    )
    adj_error, other_inputs, other_slopes = lax.optimization_barrier(
        (adj_error, other_inputs, other_slopes)
    )
    moving = ends_adj + exchange(adj_error, near).reshape(rows, channels)
    other_moving = lax.ppermute(moving, "dp", partner)
    adjoint, kernel_part = call(
        lambda *refs: final_body(scale, *refs), [result, kernels_shape],
        moving, transposed, inputs, slopes,
        scratch=[ref], flops=2 * blocks * per_conv, name="final",
    )
    other_moving, late = call(
        lambda *refs: other_body(scale, half, blocks, *refs), [plane, half_kernels],
        other_moving, transposed, other_inputs, other_slopes, kernel_part,
        scratch=[ref], flops=blocks * per_conv, name="other_late",
    )
    their_late = lax.ppermute(late, "dp", sibling)
    (early,) = call(
        lambda moving, a, b, c, d, out, ref: other_body(
            scale, 0, half, moving, a, b, c, d, None, out, ref
        ),
        [half_kernels], other_moving, transposed, other_inputs, other_slopes, kernel_part,
        scratch=[ref], flops=blocks * per_conv, name="other_early",
    )
    their_early = lax.ppermute(early, "dp", sibling)
    sums = pltpu.VMEM((half, 9 * channels, channels), f32)
    weight_grad, late_offsets = call(
        lambda mine, theirs, *refs: join_body(half, mine, theirs, None, *refs),
        [gradients, half_offsets], late, their_late,
        out_specs=[HBM, HBM], name="join_late",
        scratch=[sums, pltpu.VMEM((half, channels), f32), dma((half + 1,))],
    )
    weight_grad, bias_grad = call(
        lambda mine, theirs, offsets, _, *refs: join_body(0, mine, theirs, offsets, *refs),
        [gradients, jax.ShapeDtypeStruct((blocks, channels), f32)],
        early, their_early, late_offsets, weight_grad,
        ins=[VMEM, VMEM, VMEM, HBM], out_specs=[HBM, HBM], aliases={3: 0}, name="join_early",
        scratch=[sums, pltpu.VMEM((blocks, channels), f32), dma((half + 1,))],
    )
    dims = (1, count, height, width, channels)
    return (
        interval_ends.reshape(dims),
        adjoint.reshape(dims),
        weight_grad.reshape(blocks, 3, 3, channels, channels),
        bias_grad,
    )


def solution(mesh):
    in_specs = (
        P("dp", None, None, None),
        P("layer", None, None, None, None),
        P("layer", None),
        P("dp", None, None, None),
    )
    out_specs = (
        P("layer", "dp", None, None, None),
        P("layer", "dp", None, None, None),
        P("layer", None, None, None, None),
        P("layer", None),
    )
    return jax.shard_map(shards, mesh=mesh, in_specs=in_specs, out_specs=out_specs, check_vma=False)
```

```python
import math

import jax
import jax.numpy as jnp
from jax import lax
from jax.experimental import pallas as pl
from jax.experimental.pallas import tpu as pltpu
from jax.sharding import PartitionSpec as P

GROUP = 8
EXTRA = 8
VMEM_LIMIT = 12 * 1024 * 1024
f32 = jnp.float32
bf16 = jnp.bfloat16


def shifted_columns(value, width):
    rows = value.shape[0]
    at = lax.broadcasted_iota(jnp.int32, value.shape, 0) % width
    left = jnp.where(at == 0, 0.0, pltpu.roll(value, 1, 0))
    right = jnp.where(at == width - 1, 0.0, pltpu.roll(value, rows - 1, 0))
    return jnp.concatenate([left.astype(bf16), value.astype(bf16), right.astype(bf16)], axis=1)


def clear_border(ref):
    height = ref.shape[1]
    edge = jnp.zeros((ref.shape[0], 1) + ref.shape[2:], ref.dtype)
    ref[:, 0:1] = edge
    ref[:, height - 1 : height] = edge


def rows_from(ref, row_at):
    images, height, width, lanes = ref.shape
    return ref[:, row_at : row_at + height - 2].reshape(images * (height - 2) * width, lanes)


def convolve(ref, value, kernel):
    images, height, width, lanes = ref.shape
    rows = (height - 2) * width
    parts = []
    for image in range(images):
        moved = shifted_columns(value[image * rows : (image + 1) * rows], width)
        ref[image, 1 : height - 1] = moved.reshape(height - 2, width, lanes)
        window = [ref[image, at : at + height - 2].reshape(rows, lanes) for at in range(3)]
        parts.append(
            jnp.dot(jnp.concatenate(window, axis=1), kernel[...], preferred_element_type=f32)
        )
    return jnp.concatenate(parts, axis=0)


def split(value):
    high = value.astype(bf16)
    low = (value - high.astype(f32)).astype(bf16)
    return high, low


def times(value, matrix, transpose=False):
    dims = (((1,), (1 if transpose else 0,)), ((), ()))
    high, low = split(value)
    mhigh, mlow = split(matrix)
    dot = lambda a, b: lax.dot_general(a, b, dims, preferred_element_type=f32)
    rows = value.shape[0]
    both = dot(jnp.concatenate([high, low], axis=0), mhigh)
    return both[:rows] + (both[rows:] + dot(high, mlow))


VMEM = pl.BlockSpec(memory_space=pltpu.VMEM)
SMEM = pl.BlockSpec(memory_space=pltpu.SMEM)
HBM = pl.BlockSpec(memory_space=pltpu.HBM)


def call(body, outs, *args, ins=None, out_specs=None, scratch=(), flops=0, aliases=None, name=None):
    size = sum(a.size * a.dtype.itemsize for a in args)
    size += sum(math.prod(o.shape) * jnp.dtype(o.dtype).itemsize for o in outs)
    return pl.pallas_call(
        body,
        out_shape=tuple(outs),
        in_specs=list(ins) if ins else [VMEM] * len(args),
        out_specs=tuple(out_specs) if out_specs else (VMEM,) * len(outs),
        scratch_shapes=list(scratch),
        input_output_aliases=aliases or {},
        cost_estimate=pl.CostEstimate(flops=flops, bytes_accessed=size, transcendentals=0),
        compiler_params=pltpu.CompilerParams(vmem_limit_bytes=VMEM_LIMIT),
        name=name,
    )(*args)


def shape(dims, dtype=f32):
    return pltpu.VMEM(dims, dtype)


def stored(dims, dtype=f32):
    return pltpu.HBM(dims, dtype)


def in_hbm(value):
    return pltpu.with_memory_space_constraint(value, pltpu.HBM)


def coarse_body(weights, out, centre, sem):
    copy = pltpu.make_async_copy(weights.at[:, 4], centre, sem)
    copy.start()
    copy.wait()
    total = centre[0].astype(f32)
    for index in range(1, centre.shape[0]):
        total = total + centre[index].astype(f32)
    out[...] = 0.25 * total


def load_body(
    weights, images, biases, end_grad, weights_out, images_out, biases_out, end_out, sems
):
    pairs = [(weights, weights_out), (images, images_out), (biases, biases_out)]
    pairs.append((end_grad, end_out))
    copies = [pltpu.make_async_copy(a, b, sems.at[at]) for at, (a, b) in enumerate(pairs)]
    for copy in copies:
        copy.start()
    for copy in copies:
        copy.wait()


def flip_body(weights, transposed):
    taps, channels = weights.shape[1], weights.shape[2]
    for index in range(weights.shape[0]):
        for tap in range(taps):
            flipped = weights[index, taps - 1 - tap].astype(f32).T
            transposed[index, tap * channels : (tap + 1) * channels] = flipped.astype(bf16)


def start_body(images, own, before, weights, biases, payload, ref):
    clear_border(ref)
    field = images[...]
    state = field + times(field, before[...])
    for index in range(weights.shape[0]):
        state = state + 0.25 * jnp.tanh(
            convolve(ref, state, weights.at[index]) + biases[index : index + 1]
        )
    matrix = own[...]
    residual = state - (field + times(field, matrix))
    part = residual.shape[0] // GROUP
    for index in range(GROUP):
        payload[index, :part] = residual[index * part : (index + 1) * part]
        payload[index, part:] = matrix


def ends_body(images, end_grad, own, before, after, starts_out, ends_out, back_out):
    field = images[...]
    starts_out[...] = field + times(field, before[...])
    field = end_grad[...]
    ends_out[...] = field + times(field, after[...], True)
    back_out[...] = field + times(field, own[...], True)


def total_body(pieces, payload, locals_out):
    part = locals_out.shape[1]
    error = pieces[0, :part]
    product = pieces[0, part:]
    for index in range(1, GROUP):
        matrix = pieces[index, part:]
        locals_out[index] = error
        error = error + (times(error, matrix) + pieces[index, :part])
        product = product + (matrix + times(product, matrix))
    payload[:part] = error
    payload[part:] = product


def pair_body(part, spot, mine, theirs, out):
    upper = spot[1] == 1
    early = jnp.where(upper, theirs[...], mine[...])
    late = jnp.where(upper, mine[...], theirs[...])
    out[...] = early + (times(early, late[part:]) + late)


def back_pair_body(part, spot, mine, theirs, mine_full, theirs_full, out):
    upper = spot[1] == 1
    early = jnp.where(upper, mine[...], theirs[...])
    late = jnp.where(upper, theirs[...], mine[...])
    matrix = jnp.where(upper, theirs_full[part:], mine_full[part:])
    out[...] = early + (times(early, matrix, True) + late)


def products_body(part, pieces, prefix_out, suffix_out):
    before = pieces[0, part:]
    after = pieces[GROUP - 1, part:]
    for index in range(1, GROUP):
        prefix_out[index] = before
        suffix_out[GROUP - 1 - index] = after
        if index < GROUP - 1:
            matrix = pieces[index, part:]
            before = before + (matrix + times(before, matrix))
            matrix = pieces[GROUP - 1 - index, part:]
            after = after + (matrix + times(matrix, after))


def back_total_body(part, pieces, first, payload, locals_out):
    error = pieces[GROUP - 1]
    for index in range(GROUP - 2, -1, -1):
        locals_out[index] = error
        error = error + (times(error, first[index, part:], True) + pieces[index])
    payload[...] = error


def replay_body(
    spot, theirs, far1, far2, far3, locals_in, prefix_in, result, prefix, out, sem, sems
):
    stores = [pltpu.make_async_copy(out.at[at], result.at[at], sems.at[at]) for at in range(GROUP)]
    copy = pltpu.make_async_copy(prefix_in, prefix, sem)
    copy.start()
    part = out.shape[1]
    error = jnp.where(spot[0] >= 3, far3[:part], 0.0)
    for distance, group in ((2, far2), (1, far1)):
        longer = error + (times(error, group[part:]) + group[:part])
        error = jnp.where(spot[0] >= distance, longer, error)
    longer = error + (times(error, theirs[part:]) + theirs[:part])
    error = jnp.where(spot[1] == 1, longer, error)
    out[0] = error
    stores[0].start()
    copy.wait()
    for index in range(1, GROUP):
        out[index] = error + (times(error, prefix[index]) + locals_in[index])
        stores[index].start()
    for store in stores:
        store.wait()


def back_replay_body(
    spot, theirs, far1, far2, far3, theirs_full, full1, full2, locals_in, suffix_in,
    result, suffix, out, sem, sems,
):
    stores = [pltpu.make_async_copy(out.at[at], result.at[at], sems.at[at]) for at in range(GROUP)]
    copy = pltpu.make_async_copy(suffix_in, suffix, sem)
    copy.start()
    part = out.shape[1]
    error = far3[...]
    for group, full in ((far2, full2), (far1, full1)):
        error = error + (times(error, full[part:], True) + group[...])
    longer = error + (times(error, theirs_full[part:], True) + theirs[...])
    error = jnp.where(spot[1] == 0, longer, error)
    out[GROUP - 1] = error
    stores[GROUP - 1].start()
    copy.wait()
    for index in range(GROUP - 1):
        out[index] = error + (times(error, suffix[index], True) + locals_in[index])
        stores[index].start()
    for store in stores:
        store.wait()


def forward_sweep(state, weights, biases, ref, inputs, slopes, stores, fetches=None):
    for index in range(weights.shape[0]):
        if fetches is not None:
            fetches[index].wait()
        activation = jnp.tanh(convolve(ref, state, weights.at[index]) + biases[index : index + 1])
        channels = state.shape[1]
        inputs[index] = ref[:, :, :, channels : 2 * channels]
        slopes[index] = 0.25 * (1.0 - activation * activation)
        for store in stores[index]:
            store.start()
        state = state + 0.25 * activation
    return state


def sweep_stores(inputs, slopes, inputs_out, slopes_out, sems):
    blocks = inputs.shape[0]
    return [
        [
            pltpu.make_async_copy(inputs.at[index], inputs_out.at[index], sems.at[index]),
            pltpu.make_async_copy(slopes.at[index], slopes_out.at[index], sems.at[blocks + index]),
        ]
        for index in range(blocks)
    ]


def middle_body(
    corrected, ends_in, back_in, weights_in, transposed_in, biases_in,
    ends_out, inputs_out, slopes_out, residual_out,
    ref, ends, inputs, slopes, ends_adj, back, weights, transposed, biases, sems, loads,
):
    blocks = weights.shape[0]
    pairs = [(biases_in, biases)]
    pairs += [(weights_in.at[index], weights.at[index]) for index in range(blocks)]
    pairs += [(transposed_in, transposed), (ends_in, ends_adj), (back_in, back)]
    fetches = [pltpu.make_async_copy(a, b, loads.at[at]) for at, (a, b) in enumerate(pairs)]
    for fetch in fetches:
        fetch.start()
    clear_border(ref)
    stores = sweep_stores(inputs, slopes, inputs_out, slopes_out, sems)
    fetches[0].wait()
    ends[...] = forward_sweep(
        corrected[...], weights, biases, ref, inputs, slopes, stores, fetches[1 : 1 + blocks]
    )
    for fetch in fetches[1 + blocks :]:
        fetch.wait()
    last = pltpu.make_async_copy(ends, ends_out, sems.at[2 * blocks])
    last.start()
    adjoint = ends_adj[...]
    for index in reversed(range(blocks)):
        change = slopes[index] * adjoint
        adjoint = adjoint + convolve(ref, change, transposed.at[index])
    residual_out[...] = adjoint - back[...]
    for store in sum(stores, [last]):
        store.wait()


def again_body(corrected, weights, biases, inputs_out, slopes_out, ref, inputs, slopes, sems):
    clear_border(ref)
    stores = sweep_stores(inputs, slopes, inputs_out, slopes_out, sems)
    forward_sweep(corrected[...], weights, biases, ref, inputs, slopes, stores)
    for store in sum(stores, []):
        store.wait()


def finish_block(scale, adjoint, transposed, inputs, slope, ref):
    channels = adjoint.shape[1]
    change = slope * adjoint
    adjoint = adjoint + convolve(ref, change, transposed)
    offset = jnp.sum(change, axis=0, keepdims=True) * scale
    moved = rows_from(ref, 1)
    field = jnp.concatenate([rows_from(inputs, row_at) for row_at in range(3)], axis=1)
    kernel = scale * lax.dot_general(
        field, moved, (((0,), (0,)), ((), ())), preferred_element_type=f32
    )
    taps = [
        kernel[
            row_at * channels : (row_at + 1) * channels,
            (2 - col_at) * channels : (3 - col_at) * channels,
        ]
        for row_at in range(3)
        for col_at in range(3)
    ]
    taps.append(jnp.broadcast_to(offset, (EXTRA, channels)))
    return adjoint, jnp.concatenate(taps, axis=0)


def final_body(scale, moving, transposed, inputs, slopes, adjoint_out, kernels_out, ref):
    clear_border(ref)
    adjoint = moving[...]
    for index in reversed(range(transposed.shape[0])):
        adjoint, kernels_out[index] = finish_block(
            scale, adjoint, transposed.at[index], inputs.at[index], slopes[index], ref
        )
    adjoint_out[...] = adjoint


def other_body(
    scale, first, last, moving, transposed, inputs, slopes, kernels, adjoint_out, kernels_out, ref
):
    clear_border(ref)
    adjoint = moving[...]
    for index in reversed(range(first, last)):
        adjoint, kernel = finish_block(
            scale, adjoint, transposed.at[index], inputs.at[index], slopes[index], ref
        )
        kernels_out[index - first] = kernels[index] + kernel
    if adjoint_out is not None:
        adjoint_out[...] = adjoint


def join_body(first, mine, theirs, late, kernels_out, offsets_out, total, offsets, sems):
    size = kernels_out.shape[1]
    count = mine.shape[0]
    offsets[:count] = mine[:, size] + theirs[:, size]
    if late is not None:
        offsets[count:] = late[...]
    copies = [pltpu.make_async_copy(offsets, offsets_out, sems.at[count])]
    copies[0].start()
    for index in range(count):
        total[index] = mine[index, :size] + theirs[index, :size]
        copies.append(
            pltpu.make_async_copy(total.at[index], kernels_out.at[first + index], sems.at[index])
        )
        copies[-1].start()
    for copy in copies:
        copy.wait()


def shards(images, weights, biases, end_grad):
    count, height, width, channels = images.shape
    blocks = weights.shape[0]
    rows = count * height * width
    part = rows // GROUP
    layers = lax.axis_size("layer")
    outer = layers // GROUP
    near = [[a * GROUP + b for b in range(GROUP)] for a in range(outer)]
    pair = [(i, i ^ GROUP) for i in range(layers)]
    around = [[(i, (i + 2 * GROUP * d) % layers) for i in range(layers)] for d in (1, 2, 3)]
    down = [[(i, i - 2 * GROUP * d) for i in range(2 * GROUP * d, layers)] for d in (1, 2, 3)]
    dp = lax.axis_size("dp")
    partner = [(i, (i + dp // 2) % dp) for i in range(dp)]
    sibling = [(i, i ^ 1) for i in range(dp)]
    spot = lax.axis_index("layer").astype(jnp.int32)
    spot = jnp.stack([spot >> 4, (spot >> 3) & 1])
    scale = 1.0 / (count * dp)
    per_conv = 2 * rows * 9 * channels * channels
    half = blocks // 2

    def exchange(value, groups):
        return lax.all_to_all(value, "layer", 0, 0, axis_index_groups=groups)

    plane = shape((rows, channels))
    kept = stored((rows, channels))
    matrix = shape((channels, channels))
    pieces_shape = shape((GROUP, part, channels))
    pieces_kept = stored((GROUP, part, channels))
    both_kept = stored((GROUP, part + channels, channels))
    both = shape((part + channels, channels))
    piece = shape((part, channels))
    matrices = stored((GROUP, channels, channels))
    taps_shape = shape((blocks, 9, channels, channels), bf16)
    sweep_shape = (blocks, 9 * channels, channels)
    inputs_dims = (blocks, count, height + 2, width, channels)
    slopes_dims = (blocks, rows, channels)
    offsets_shape = shape((blocks, channels))
    kernels_shape = shape((blocks, 9 * channels + EXTRA, channels))
    half_kernels = shape((half, 9 * channels + EXTRA, channels))
    result = jax.ShapeDtypeStruct((rows, channels), f32)
    gradients = jax.ShapeDtypeStruct((blocks, 9 * channels, channels), f32)
    half_offsets = jax.ShapeDtypeStruct((half, channels), f32)
    ref = pltpu.VMEM((count, height + 2, width, 3 * channels), bf16)
    dma = pltpu.SemaphoreType.DMA
    sweep_scratch = [pltpu.VMEM(inputs_dims, bf16), pltpu.VMEM(slopes_dims, f32)]

    flat = weights.reshape(blocks, 9, channels, channels)
    kernels = weights.reshape(sweep_shape)
    (own,) = call(
        coarse_body, [matrix], in_hbm(flat), ins=[HBM],
        scratch=[pltpu.VMEM((blocks, channels, channels), bf16), dma(())], name="coarse",
    )
    before = lax.ppermute(own, "layer", [(i, i + 1) for i in range(layers - 1)])
    after = lax.ppermute(own, "layer", [(i + 1, i) for i in range(layers - 1)])
    held, field, offsets, cotangent = call(
        load_body, [taps_shape, plane, offsets_shape, plane],
        in_hbm(flat), in_hbm(images.reshape(rows, channels)), in_hbm(biases),
        in_hbm(end_grad.reshape(rows, channels)),
        ins=[HBM] * 4, scratch=[dma((4,))], name="load",
    )

    (payload,) = call(
        start_body, [both_kept], field, own, before, held.reshape(sweep_shape), offsets,
        scratch=[ref], flops=blocks * per_conv, name="start",
    )
    first = exchange(payload, near)
    first, after = lax.optimization_barrier((first, after))
    starts, ends_adj, back = call(
        ends_body, [kept] * 3, field, cotangent, own, before, after, name="ends"
    )
    (transposed,) = call(flip_body, [stored(sweep_shape, bf16)], flat, name="flip")
    first, transposed = lax.optimization_barrier((first, transposed))
    full, prefixes = call(total_body, [both, pieces_shape], first, name="total")
    their_full = lax.ppermute(full, "layer", pair)
    (pair_full,) = call(
        lambda *refs: pair_body(part, *refs), [both], spot, full, their_full,
        ins=[SMEM, VMEM, VMEM], name="pair",
    )
    around_full = [lax.ppermute(pair_full, "layer", to) for to in around]
    prefix, suffix = call(
        lambda *refs: products_body(part, *refs), [matrices] * 2, first, name="products"
    )
    replay_scratch = [
        pltpu.VMEM((GROUP, channels, channels), f32), pltpu.VMEM((GROUP, part, channels), f32),
        dma(()), dma((GROUP,)),
    ]
    (error,) = call(
        replay_body, [pieces_kept], spot, their_full, *around_full, prefixes, in_hbm(prefix),
        ins=[SMEM] + [VMEM] * 5 + [HBM], out_specs=[HBM], scratch=replay_scratch, name="replay",
    )
    error, suffix, starts, ends_adj, back = lax.optimization_barrier(
        (error, suffix, starts, ends_adj, back)
    )
    corrected = starts + exchange(error, near).reshape(rows, channels)
    other_corrected = lax.ppermute(corrected, "dp", partner)

    interval_ends, inputs, slopes, adj_residual = call(
        middle_body, [result, stored(inputs_dims, bf16), stored(slopes_dims), kept],
        corrected, in_hbm(ends_adj), in_hbm(back), in_hbm(kernels),
        in_hbm(transposed), in_hbm(biases),
        ins=[VMEM] + [HBM] * 5, out_specs=[HBM, HBM, HBM, VMEM],
        scratch=[ref, pltpu.VMEM((rows, channels), f32)] + sweep_scratch
        + [pltpu.VMEM((rows, channels), f32)] * 2 + [pltpu.VMEM(sweep_shape, bf16)] * 2
        + [pltpu.VMEM((blocks, channels), f32), dma((2 * blocks + 1,)), dma((blocks + 4,))],
        flops=2 * blocks * per_conv, name="middle",
    )
    pieces = exchange(adj_residual.reshape(GROUP, part, channels), near)
    total, prefixes = call(
        lambda *refs: back_total_body(part, *refs), [piece, pieces_kept], pieces, first,
        name="back_total",
    )
    their_total = lax.ppermute(total, "layer", pair)
    (pair_total,) = call(
        lambda *refs: back_pair_body(part, *refs), [piece],
        spot, total, their_total, full, their_full, ins=[SMEM] + [VMEM] * 4, name="back_pair",
    )
    down_total = [lax.ppermute(pair_total, "layer", to) for to in down]
    other_inputs, other_slopes = call(
        again_body, [stored(inputs_dims, bf16), stored(slopes_dims)],
        other_corrected, kernels, offsets, out_specs=[HBM] * 2,
        scratch=[ref] + sweep_scratch + [dma((2 * blocks,))], flops=blocks * per_conv, name="again",
    )
    (adj_error,) = call(
        back_replay_body, [pieces_kept], spot, their_total, *down_total, their_full,
        around_full[2], around_full[1], prefixes, in_hbm(suffix),
        ins=[SMEM] + [VMEM] * 8 + [HBM], out_specs=[HBM], scratch=replay_scratch,
        name="back_replay",
    )
    adj_error, other_inputs, other_slopes = lax.optimization_barrier(
        (adj_error, other_inputs, other_slopes)
    )
    moving = ends_adj + exchange(adj_error, near).reshape(rows, channels)
    other_moving = lax.ppermute(moving, "dp", partner)
    adjoint, kernel_part = call(
        lambda *refs: final_body(scale, *refs), [result, kernels_shape],
        moving, transposed, inputs, slopes,
        scratch=[ref], flops=2 * blocks * per_conv, name="final",
    )
    other_moving, late = call(
        lambda *refs: other_body(scale, half, blocks, *refs), [plane, half_kernels],
        other_moving, transposed, other_inputs, other_slopes, kernel_part,
        scratch=[ref], flops=blocks * per_conv, name="other_late",
    )
    their_late = lax.ppermute(late, "dp", sibling)
    (early,) = call(
        lambda moving, a, b, c, d, out, ref: other_body(
            scale, 0, half, moving, a, b, c, d, None, out, ref
        ),
        [half_kernels], other_moving, transposed, other_inputs, other_slopes, kernel_part,
        scratch=[ref], flops=blocks * per_conv, name="other_early",
    )
    their_early = lax.ppermute(early, "dp", sibling)
    sums = pltpu.VMEM((half, 9 * channels, channels), f32)
    weight_grad, late_offsets = call(
        lambda mine, theirs, *refs: join_body(half, mine, theirs, None, *refs),
        [gradients, half_offsets], late, their_late,
        out_specs=[HBM, HBM], name="join_late",
        scratch=[sums, pltpu.VMEM((half, channels), f32), dma((half + 1,))],
    )
    weight_grad, bias_grad = call(
        lambda mine, theirs, offsets, _, *refs: join_body(0, mine, theirs, offsets, *refs),
        [gradients, jax.ShapeDtypeStruct((blocks, channels), f32)],
        early, their_early, late_offsets, weight_grad,
        ins=[VMEM, VMEM, VMEM, HBM], out_specs=[HBM, HBM], aliases={3: 0}, name="join_early",
        scratch=[sums, pltpu.VMEM((blocks, channels), f32), dma((half + 1,))],
    )
    dims = (1, count, height, width, channels)
    return (
        interval_ends.reshape(dims),
        adjoint.reshape(dims),
        weight_grad.reshape(blocks, 3, 3, channels, channels),
        bias_grad,
    )


def solution(mesh):
    in_specs = (
        P("dp", None, None, None),
        P("layer", None, None, None, None),
        P("layer", None),
        P("dp", None, None, None),
    )
    out_specs = (
        P("layer", "dp", None, None, None),
        P("layer", "dp", None, None, None),
        P("layer", None, None, None, None),
        P("layer", None),
    )
    return jax.shard_map(shards, mesh=mesh, in_specs=in_specs, out_specs=out_specs, check_vma=False)
```

```python
import math

import jax
import jax.numpy as jnp
from jax import lax
from jax.experimental import pallas as pl
from jax.experimental.pallas import tpu as pltpu
from jax.sharding import PartitionSpec as P

GROUP = 8
EXTRA = 8
VMEM_LIMIT = 12 * 1024 * 1024
f32 = jnp.float32
bf16 = jnp.bfloat16


def shifted_columns(value, width):
    rows = value.shape[0]
    at = lax.broadcasted_iota(jnp.int32, value.shape, 0) % width
    left = jnp.where(at == 0, 0.0, pltpu.roll(value, 1, 0))
    right = jnp.where(at == width - 1, 0.0, pltpu.roll(value, rows - 1, 0))
    return jnp.concatenate([left.astype(bf16), value.astype(bf16), right.astype(bf16)], axis=1)


def clear_border(ref):
    height = ref.shape[1]
    edge = jnp.zeros((ref.shape[0], 1) + ref.shape[2:], ref.dtype)
    ref[:, 0:1] = edge
    ref[:, height - 1 : height] = edge


def rows_from(ref, row_at):
    images, height, width, lanes = ref.shape
    return ref[:, row_at : row_at + height - 2].reshape(images * (height - 2) * width, lanes)


def convolve(ref, value, kernel):
    images, height, width, lanes = ref.shape
    rows = (height - 2) * width
    parts = []
    for image in range(images):
        moved = shifted_columns(value[image * rows : (image + 1) * rows], width)
        ref[image, 1 : height - 1] = moved.reshape(height - 2, width, lanes)
        window = [ref[image, at : at + height - 2].reshape(rows, lanes) for at in range(3)]
        parts.append(
            jnp.dot(jnp.concatenate(window, axis=1), kernel[...], preferred_element_type=f32)
        )
    return jnp.concatenate(parts, axis=0)


def split(value):
    high = value.astype(bf16)
    low = (value - high.astype(f32)).astype(bf16)
    return high, low


def times(value, matrix, transpose=False):
    dims = (((1,), (1 if transpose else 0,)), ((), ()))
    high, low = split(value)
    mhigh, mlow = split(matrix)
    dot = lambda a, b: lax.dot_general(a, b, dims, preferred_element_type=f32)
    rows = value.shape[0]
    both = dot(jnp.concatenate([high, low], axis=0), mhigh)
    return both[:rows] + (both[rows:] + dot(high, mlow))


VMEM = pl.BlockSpec(memory_space=pltpu.VMEM)
SMEM = pl.BlockSpec(memory_space=pltpu.SMEM)
HBM = pl.BlockSpec(memory_space=pltpu.HBM)


def call(body, outs, *args, ins=None, out_specs=None, scratch=(), flops=0, aliases=None, name=None):
    size = sum(a.size * a.dtype.itemsize for a in args)
    size += sum(math.prod(o.shape) * jnp.dtype(o.dtype).itemsize for o in outs)
    return pl.pallas_call(
        body,
        out_shape=tuple(outs),
        in_specs=list(ins) if ins else [VMEM] * len(args),
        out_specs=tuple(out_specs) if out_specs else (VMEM,) * len(outs),
        scratch_shapes=list(scratch),
        input_output_aliases=aliases or {},
        cost_estimate=pl.CostEstimate(flops=flops, bytes_accessed=size, transcendentals=0),
        compiler_params=pltpu.CompilerParams(vmem_limit_bytes=VMEM_LIMIT),
        name=name,
    )(*args)


def shape(dims, dtype=f32):
    return pltpu.VMEM(dims, dtype)


def stored(dims, dtype=f32):
    return pltpu.HBM(dims, dtype)


def in_hbm(value):
    return pltpu.with_memory_space_constraint(value, pltpu.HBM)


def coarse_body(weights, out, centre, sem):
    copy = pltpu.make_async_copy(weights.at[:, 4], centre, sem)
    copy.start()
    copy.wait()
    total = centre[0].astype(f32)
    for index in range(1, centre.shape[0]):
        total = total + centre[index].astype(f32)
    out[...] = 0.25 * total


def load_body(
    weights, images, biases, end_grad, weights_out, images_out, biases_out, end_out, sems
):
    pairs = [(weights, weights_out), (images, images_out), (biases, biases_out)]
    pairs.append((end_grad, end_out))
    copies = [pltpu.make_async_copy(a, b, sems.at[at]) for at, (a, b) in enumerate(pairs)]
    for copy in copies:
        copy.start()
    for copy in copies:
        copy.wait()


def flip_body(weights, transposed):
    taps, channels = weights.shape[1], weights.shape[2]
    for index in range(weights.shape[0]):
        for tap in range(taps):
            flipped = weights[index, taps - 1 - tap].astype(f32).T
            transposed[index, tap * channels : (tap + 1) * channels] = flipped.astype(bf16)


def start_body(images, own, before, weights, biases, payload, ref):
    clear_border(ref)
    field = images[...]
    state = field + times(field, before[...])
    for index in range(weights.shape[0]):
        state = state + 0.25 * jnp.tanh(
            convolve(ref, state, weights.at[index]) + biases[index : index + 1]
        )
    matrix = own[...]
    residual = state - (field + times(field, matrix))
    part = residual.shape[0] // GROUP
    for index in range(GROUP):
        payload[index, :part] = residual[index * part : (index + 1) * part]
        payload[index, part:] = matrix


def ends_body(images, end_grad, own, before, after, starts_out, ends_out, back_out):
    field = images[...]
    starts_out[...] = field + times(field, before[...])
    field = end_grad[...]
    ends_out[...] = field + times(field, after[...], True)
    back_out[...] = field + times(field, own[...], True)


def total_body(pieces, payload, locals_out):
    part = locals_out.shape[1]
    error = pieces[0, :part]
    product = pieces[0, part:]
    for index in range(1, GROUP):
        matrix = pieces[index, part:]
        locals_out[index] = error
        error = error + (times(error, matrix) + pieces[index, :part])
        product = product + (matrix + times(product, matrix))
    payload[:part] = error
    payload[part:] = product


def pair_body(part, spot, mine, theirs, out):
    upper = spot[1] == 1
    early = jnp.where(upper, theirs[...], mine[...])
    late = jnp.where(upper, mine[...], theirs[...])
    out[...] = early + (times(early, late[part:]) + late)


def back_pair_body(part, spot, mine, theirs, mine_full, theirs_full, out):
    upper = spot[1] == 1
    early = jnp.where(upper, mine[...], theirs[...])
    late = jnp.where(upper, theirs[...], mine[...])
    matrix = jnp.where(upper, theirs_full[part:], mine_full[part:])
    out[...] = early + (times(early, matrix, True) + late)


def products_body(part, pieces, prefix_out, suffix_out):
    before = pieces[0, part:]
    after = pieces[GROUP - 1, part:]
    for index in range(1, GROUP):
        prefix_out[index] = before
        suffix_out[GROUP - 1 - index] = after
        if index < GROUP - 1:
            matrix = pieces[index, part:]
            before = before + (matrix + times(before, matrix))
            matrix = pieces[GROUP - 1 - index, part:]
            after = after + (matrix + times(matrix, after))


def back_total_body(part, pieces, first, payload, locals_out):
    error = pieces[GROUP - 1]
    for index in range(GROUP - 2, -1, -1):
        locals_out[index] = error
        error = error + (times(error, first[index, part:], True) + pieces[index])
    payload[...] = error


def replay_body(
    spot, theirs, far1, far2, far3, locals_in, prefix_in, result, prefix, out, sem, sems
):
    stores = [pltpu.make_async_copy(out.at[at], result.at[at], sems.at[at]) for at in range(GROUP)]
    copy = pltpu.make_async_copy(prefix_in, prefix, sem)
    copy.start()
    part = out.shape[1]
    error = jnp.where(spot[0] >= 3, far3[:part], 0.0)
    for distance, group in ((2, far2), (1, far1)):
        longer = error + (times(error, group[part:]) + group[:part])
        error = jnp.where(spot[0] >= distance, longer, error)
    longer = error + (times(error, theirs[part:]) + theirs[:part])
    error = jnp.where(spot[1] == 1, longer, error)
    out[0] = error
    stores[0].start()
    copy.wait()
    for index in range(1, GROUP):
        out[index] = error + (times(error, prefix[index]) + locals_in[index])
        stores[index].start()
    for store in stores:
        store.wait()


def back_replay_body(
    spot, theirs, far1, far2, far3, theirs_full, full1, full2, locals_in, suffix_in,
    result, suffix, out, sem, sems,
):
    stores = [pltpu.make_async_copy(out.at[at], result.at[at], sems.at[at]) for at in range(GROUP)]
    copy = pltpu.make_async_copy(suffix_in, suffix, sem)
    copy.start()
    part = out.shape[1]
    error = far3[...]
    for group, full in ((far2, full2), (far1, full1)):
        error = error + (times(error, full[part:], True) + group[...])
    longer = error + (times(error, theirs_full[part:], True) + theirs[...])
    error = jnp.where(spot[1] == 0, longer, error)
    out[GROUP - 1] = error
    stores[GROUP - 1].start()
    copy.wait()
    for index in range(GROUP - 1):
        out[index] = error + (times(error, suffix[index], True) + locals_in[index])
        stores[index].start()
    for store in stores:
        store.wait()


def forward_sweep(state, weights, biases, ref, inputs, slopes, stores, fetches=None):
    for index in range(weights.shape[0]):
        if fetches is not None:
            fetches[index].wait()
        activation = jnp.tanh(convolve(ref, state, weights.at[index]) + biases[index : index + 1])
        channels = state.shape[1]
        inputs[index] = ref[:, :, :, channels : 2 * channels]
        slopes[index] = 0.25 * (1.0 - activation * activation)
        for store in stores[index]:
            store.start()
        state = state + 0.25 * activation
    return state


def sweep_stores(inputs, slopes, inputs_out, slopes_out, sems):
    blocks = inputs.shape[0]
    return [
        [
            pltpu.make_async_copy(inputs.at[index], inputs_out.at[index], sems.at[index]),
            pltpu.make_async_copy(slopes.at[index], slopes_out.at[index], sems.at[blocks + index]),
        ]
        for index in range(blocks)
    ]


def middle_body(
    corrected, ends_in, back_in, weights_in, transposed_in, biases_in,
    ends_out, inputs_out, slopes_out, residual_out,
    ref, ends, inputs, slopes, ends_adj, back, weights, transposed, biases, sems, loads,
):
    blocks = weights.shape[0]
    pairs = [(biases_in, biases)]
    pairs += [(weights_in.at[index], weights.at[index]) for index in range(blocks)]
    pairs += [(transposed_in, transposed), (ends_in, ends_adj), (back_in, back)]
    fetches = [pltpu.make_async_copy(a, b, loads.at[at]) for at, (a, b) in enumerate(pairs)]
    for fetch in fetches:
        fetch.start()
    clear_border(ref)
    stores = sweep_stores(inputs, slopes, inputs_out, slopes_out, sems)
    fetches[0].wait()
    ends[...] = forward_sweep(
        corrected[...], weights, biases, ref, inputs, slopes, stores, fetches[1 : 1 + blocks]
    )
    for fetch in fetches[1 + blocks :]:
        fetch.wait()
    last = pltpu.make_async_copy(ends, ends_out, sems.at[2 * blocks])
    last.start()
    adjoint = ends_adj[...]
    for index in reversed(range(blocks)):
        change = slopes[index] * adjoint
        adjoint = adjoint + convolve(ref, change, transposed.at[index])
    residual_out[...] = adjoint - back[...]
    for store in sum(stores, [last]):
        store.wait()


def again_body(corrected, weights, biases, inputs_out, slopes_out, ref, inputs, slopes, sems):
    clear_border(ref)
    stores = sweep_stores(inputs, slopes, inputs_out, slopes_out, sems)
    forward_sweep(corrected[...], weights, biases, ref, inputs, slopes, stores)
    for store in sum(stores, []):
        store.wait()


def finish_block(scale, adjoint, transposed, inputs, slope, ref):
    channels = adjoint.shape[1]
    change = slope * adjoint
    adjoint = adjoint + convolve(ref, change, transposed)
    offset = jnp.sum(change, axis=0, keepdims=True) * scale
    moved = rows_from(ref, 1)
    field = jnp.concatenate([rows_from(inputs, row_at) for row_at in range(3)], axis=1)
    kernel = scale * lax.dot_general(
        field, moved, (((0,), (0,)), ((), ())), preferred_element_type=f32
    )
    taps = [
        kernel[
            row_at * channels : (row_at + 1) * channels,
            (2 - col_at) * channels : (3 - col_at) * channels,
        ]
        for row_at in range(3)
        for col_at in range(3)
    ]
    taps.append(jnp.broadcast_to(offset, (EXTRA, channels)))
    return adjoint, jnp.concatenate(taps, axis=0)


def final_body(scale, moving, transposed, inputs, slopes, adjoint_out, kernels_out, ref):
    clear_border(ref)
    adjoint = moving[...]
    for index in reversed(range(transposed.shape[0])):
        adjoint, kernels_out[index] = finish_block(
            scale, adjoint, transposed.at[index], inputs.at[index], slopes[index], ref
        )
    adjoint_out[...] = adjoint


def other_body(
    scale, first, last, moving, transposed, inputs, slopes, kernels, adjoint_out, kernels_out, ref
):
    clear_border(ref)
    adjoint = moving[...]
    for index in reversed(range(first, last)):
        adjoint, kernel = finish_block(
            scale, adjoint, transposed.at[index], inputs.at[index], slopes[index], ref
        )
        kernels_out[index - first] = kernels[index] + kernel
    if adjoint_out is not None:
        adjoint_out[...] = adjoint


def join_body(first, mine, theirs, late, kernels_out, offsets_out, total, offsets, sems):
    size = kernels_out.shape[1]
    count = mine.shape[0]
    offsets[:count] = mine[:, size] + theirs[:, size]
    if late is not None:
        offsets[count:] = late[...]
    copies = [pltpu.make_async_copy(offsets, offsets_out, sems.at[count])]
    copies[0].start()
    for index in range(count):
        total[index] = mine[index, :size] + theirs[index, :size]
        copies.append(
            pltpu.make_async_copy(total.at[index], kernels_out.at[first + index], sems.at[index])
        )
        copies[-1].start()
    for copy in copies:
        copy.wait()


def shards(images, weights, biases, end_grad):
    count, height, width, channels = images.shape
    blocks = weights.shape[0]
    rows = count * height * width
    part = rows // GROUP
    layers = lax.axis_size("layer")
    outer = layers // GROUP
    near = [[a * GROUP + b for b in range(GROUP)] for a in range(outer)]
    pair = [(i, i ^ GROUP) for i in range(layers)]
    around = [[(i, (i + 2 * GROUP * d) % layers) for i in range(layers)] for d in (1, 2, 3)]
    down = [[(i, i - 2 * GROUP * d) for i in range(2 * GROUP * d, layers)] for d in (1, 2, 3)]
    dp = lax.axis_size("dp")
    partner = [(i, (i + dp // 2) % dp) for i in range(dp)]
    sibling = [(i, i ^ 1) for i in range(dp)]
    spot = lax.axis_index("layer").astype(jnp.int32)
    spot = jnp.stack([spot >> 4, (spot >> 3) & 1])
    scale = 1.0 / (count * dp)
    per_conv = 2 * rows * 9 * channels * channels
    half = blocks // 2

    def exchange(value, groups):
        return lax.all_to_all(value, "layer", 0, 0, axis_index_groups=groups)

    plane = shape((rows, channels))
    kept = stored((rows, channels))
    matrix = shape((channels, channels))
    pieces_shape = shape((GROUP, part, channels))
    pieces_kept = stored((GROUP, part, channels))
    both_kept = stored((GROUP, part + channels, channels))
    both = shape((part + channels, channels))
    piece = shape((part, channels))
    matrices = stored((GROUP, channels, channels))
    taps_shape = shape((blocks, 9, channels, channels), bf16)
    sweep_shape = (blocks, 9 * channels, channels)
    inputs_dims = (blocks, count, height + 2, width, channels)
    slopes_dims = (blocks, rows, channels)
    offsets_shape = shape((blocks, channels))
    kernels_shape = shape((blocks, 9 * channels + EXTRA, channels))
    half_kernels = shape((half, 9 * channels + EXTRA, channels))
    result = jax.ShapeDtypeStruct((rows, channels), f32)
    gradients = jax.ShapeDtypeStruct((blocks, 9 * channels, channels), f32)
    half_offsets = jax.ShapeDtypeStruct((half, channels), f32)
    ref = pltpu.VMEM((count, height + 2, width, 3 * channels), bf16)
    dma = pltpu.SemaphoreType.DMA
    sweep_scratch = [pltpu.VMEM(inputs_dims, bf16), pltpu.VMEM(slopes_dims, f32)]

    flat = weights.reshape(blocks, 9, channels, channels)
    kernels = weights.reshape(sweep_shape)
    (own,) = call(
        coarse_body, [matrix], in_hbm(flat), ins=[HBM],
        scratch=[pltpu.VMEM((blocks, channels, channels), bf16), dma(())], name="coarse",
    )
    before = lax.ppermute(own, "layer", [(i, i + 1) for i in range(layers - 1)])
    after = lax.ppermute(own, "layer", [(i + 1, i) for i in range(layers - 1)])
    held, field, offsets, cotangent = call(
        load_body, [taps_shape, plane, offsets_shape, plane],
        in_hbm(flat), in_hbm(images.reshape(rows, channels)), in_hbm(biases),
        in_hbm(end_grad.reshape(rows, channels)),
        ins=[HBM] * 4, scratch=[dma((4,))], name="load",
    )

    (payload,) = call(
        start_body, [both_kept], field, own, before, held.reshape(sweep_shape), offsets,
        scratch=[ref], flops=blocks * per_conv, name="start",
    )
    first = exchange(payload, near)
    first, after = lax.optimization_barrier((first, after))
    starts, ends_adj, back = call(
        ends_body, [kept] * 3, field, cotangent, own, before, after, name="ends"
    )
    (transposed,) = call(flip_body, [stored(sweep_shape, bf16)], flat, name="flip")
    first, transposed = lax.optimization_barrier((first, transposed))
    full, prefixes = call(total_body, [both, pieces_shape], first, name="total")
    their_full = lax.ppermute(full, "layer", pair)
    (pair_full,) = call(
        lambda *refs: pair_body(part, *refs), [both], spot, full, their_full,
        ins=[SMEM, VMEM, VMEM], name="pair",
    )
    around_full = [lax.ppermute(pair_full, "layer", to) for to in around]
    prefix, suffix = call(
        lambda *refs: products_body(part, *refs), [matrices] * 2, first, name="products"
    )
    replay_scratch = [
        pltpu.VMEM((GROUP, channels, channels), f32), pltpu.VMEM((GROUP, part, channels), f32),
        dma(()), dma((GROUP,)),
    ]
    (error,) = call(
        replay_body, [pieces_kept], spot, their_full, *around_full, prefixes, in_hbm(prefix),
        ins=[SMEM] + [VMEM] * 5 + [HBM], out_specs=[HBM], scratch=replay_scratch, name="replay",
    )
    error, suffix, starts, ends_adj, back = lax.optimization_barrier(
        (error, suffix, starts, ends_adj, back)
    )
    corrected = starts + exchange(error, near).reshape(rows, channels)

    interval_ends, inputs, slopes, adj_residual = call(
        middle_body, [result, stored(inputs_dims, bf16), stored(slopes_dims), kept],
        corrected, in_hbm(ends_adj), in_hbm(back), in_hbm(kernels),
        in_hbm(transposed), in_hbm(biases),
        ins=[VMEM] + [HBM] * 5, out_specs=[HBM, HBM, HBM, VMEM],
        scratch=[ref, pltpu.VMEM((rows, channels), f32)] + sweep_scratch
        + [pltpu.VMEM((rows, channels), f32)] * 2 + [pltpu.VMEM(sweep_shape, bf16)] * 2
        + [pltpu.VMEM((blocks, channels), f32), dma((2 * blocks + 1,)), dma((blocks + 4,))],
        flops=2 * blocks * per_conv, name="middle",
    )
    pieces = exchange(adj_residual.reshape(GROUP, part, channels), near)
    total, prefixes = call(
        lambda *refs: back_total_body(part, *refs), [piece, pieces_shape], pieces, first,
        name="back_total",
    )
    their_total = lax.ppermute(total, "layer", pair)
    their_total, corrected = lax.optimization_barrier((their_total, corrected))
    other_corrected = lax.ppermute(corrected, "dp", partner)
    (pair_total,) = call(
        lambda *refs: back_pair_body(part, *refs), [piece],
        spot, total, their_total, full, their_full, ins=[SMEM] + [VMEM] * 4, name="back_pair",
    )
    down_total = [lax.ppermute(pair_total, "layer", to) for to in down]
    (adj_error,) = call(
        back_replay_body, [pieces_kept], spot, their_total, *down_total, their_full,
        around_full[2], around_full[1], prefixes, in_hbm(suffix),
        ins=[SMEM] + [VMEM] * 8 + [HBM], out_specs=[HBM], scratch=replay_scratch,
        name="back_replay",
    )
    adj_error, other_corrected = lax.optimization_barrier((adj_error, other_corrected))
    other_inputs, other_slopes = call(
        again_body, [stored(inputs_dims, bf16), stored(slopes_dims)],
        other_corrected, kernels, offsets, out_specs=[HBM] * 2,
        scratch=[ref] + sweep_scratch + [dma((2 * blocks,))], flops=blocks * per_conv, name="again",
    )
    moving = ends_adj + exchange(adj_error, near).reshape(rows, channels)
    other_moving = lax.ppermute(moving, "dp", partner)
    adjoint, kernel_part = call(
        lambda *refs: final_body(scale, *refs), [result, kernels_shape],
        moving, transposed, inputs, slopes,
        scratch=[ref], flops=2 * blocks * per_conv, name="final",
    )
    other_moving, late = call(
        lambda *refs: other_body(scale, half, blocks, *refs), [plane, half_kernels],
        other_moving, transposed, other_inputs, other_slopes, kernel_part,
        scratch=[ref], flops=blocks * per_conv, name="other_late",
    )
    their_late = lax.ppermute(late, "dp", sibling)
    (early,) = call(
        lambda moving, a, b, c, d, out, ref: other_body(
            scale, 0, half, moving, a, b, c, d, None, out, ref
        ),
        [half_kernels], other_moving, transposed, other_inputs, other_slopes, kernel_part,
        scratch=[ref], flops=blocks * per_conv, name="other_early",
    )
    their_early = lax.ppermute(early, "dp", sibling)
    sums = pltpu.VMEM((half, 9 * channels, channels), f32)
    weight_grad, late_offsets = call(
        lambda mine, theirs, *refs: join_body(half, mine, theirs, None, *refs),
        [gradients, half_offsets], late, their_late,
        out_specs=[HBM, HBM], name="join_late",
        scratch=[sums, pltpu.VMEM((half, channels), f32), dma((half + 1,))],
    )
    weight_grad, bias_grad = call(
        lambda mine, theirs, offsets, _, *refs: join_body(0, mine, theirs, offsets, *refs),
        [gradients, jax.ShapeDtypeStruct((blocks, channels), f32)],
        early, their_early, late_offsets, weight_grad,
        ins=[VMEM, VMEM, VMEM, HBM], out_specs=[HBM, HBM], aliases={3: 0}, name="join_early",
        scratch=[sums, pltpu.VMEM((blocks, channels), f32), dma((half + 1,))],
    )
    dims = (1, count, height, width, channels)
    return (
        interval_ends.reshape(dims),
        adjoint.reshape(dims),
        weight_grad.reshape(blocks, 3, 3, channels, channels),
        bias_grad,
    )


def solution(mesh):
    in_specs = (
        P("dp", None, None, None),
        P("layer", None, None, None, None),
        P("layer", None),
        P("dp", None, None, None),
    )
    out_specs = (
        P("layer", "dp", None, None, None),
        P("layer", "dp", None, None, None),
        P("layer", None, None, None, None),
        P("layer", None),
    )
    return jax.shard_map(shards, mesh=mesh, in_specs=in_specs, out_specs=out_specs, check_vma=False)
```

```python
import math

import jax
import jax.numpy as jnp
from jax import lax
from jax.experimental import pallas as pl
from jax.experimental.pallas import tpu as pltpu
from jax.sharding import PartitionSpec as P

GROUP = 8
EXTRA = 8
VMEM_LIMIT = 12 * 1024 * 1024
f32 = jnp.float32
bf16 = jnp.bfloat16


def shifted_columns(value, width):
    rows = value.shape[0]
    at = lax.broadcasted_iota(jnp.int32, value.shape, 0) % width
    left = jnp.where(at == 0, 0.0, pltpu.roll(value, 1, 0))
    right = jnp.where(at == width - 1, 0.0, pltpu.roll(value, rows - 1, 0))
    return jnp.concatenate([left.astype(bf16), value.astype(bf16), right.astype(bf16)], axis=1)


def clear_border(ref):
    height = ref.shape[1]
    edge = jnp.zeros((ref.shape[0], 1) + ref.shape[2:], ref.dtype)
    ref[:, 0:1] = edge
    ref[:, height - 1 : height] = edge


def rows_from(ref, row_at):
    images, height, width, lanes = ref.shape
    return ref[:, row_at : row_at + height - 2].reshape(images * (height - 2) * width, lanes)


def convolve(ref, value, kernel):
    images, height, width, lanes = ref.shape
    rows = (height - 2) * width
    parts = []
    for image in range(images):
        moved = shifted_columns(value[image * rows : (image + 1) * rows], width)
        ref[image, 1 : height - 1] = moved.reshape(height - 2, width, lanes)
        window = [ref[image, at : at + height - 2].reshape(rows, lanes) for at in range(3)]
        parts.append(
            jnp.dot(jnp.concatenate(window, axis=1), kernel[...], preferred_element_type=f32)
        )
    return jnp.concatenate(parts, axis=0)


def split(value):
    high = value.astype(bf16)
    low = (value - high.astype(f32)).astype(bf16)
    return high, low


def times(value, matrix, transpose=False):
    dims = (((1,), (1 if transpose else 0,)), ((), ()))
    high, low = split(value)
    mhigh, mlow = split(matrix)
    dot = lambda a, b: lax.dot_general(a, b, dims, preferred_element_type=f32)
    rows = value.shape[0]
    both = dot(jnp.concatenate([high, low], axis=0), mhigh)
    return both[:rows] + (both[rows:] + dot(high, mlow))


VMEM = pl.BlockSpec(memory_space=pltpu.VMEM)
SMEM = pl.BlockSpec(memory_space=pltpu.SMEM)
HBM = pl.BlockSpec(memory_space=pltpu.HBM)


def call(body, outs, *args, ins=None, out_specs=None, scratch=(), flops=0, aliases=None, name=None):
    size = sum(a.size * a.dtype.itemsize for a in args)
    size += sum(math.prod(o.shape) * jnp.dtype(o.dtype).itemsize for o in outs)
    return pl.pallas_call(
        body,
        out_shape=tuple(outs),
        in_specs=list(ins) if ins else [VMEM] * len(args),
        out_specs=tuple(out_specs) if out_specs else (VMEM,) * len(outs),
        scratch_shapes=list(scratch),
        input_output_aliases=aliases or {},
        cost_estimate=pl.CostEstimate(flops=flops, bytes_accessed=size, transcendentals=0),
        compiler_params=pltpu.CompilerParams(vmem_limit_bytes=VMEM_LIMIT),
        name=name,
    )(*args)


def shape(dims, dtype=f32):
    return pltpu.VMEM(dims, dtype)


def stored(dims, dtype=f32):
    return pltpu.HBM(dims, dtype)


def in_hbm(value):
    return pltpu.with_memory_space_constraint(value, pltpu.HBM)


def coarse_body(weights, out, centre, sem):
    copy = pltpu.make_async_copy(weights.at[:, 4], centre, sem)
    copy.start()
    copy.wait()
    total = centre[0].astype(f32)
    for index in range(1, centre.shape[0]):
        total = total + centre[index].astype(f32)
    out[...] = 0.25 * total


def load_body(
    weights, images, biases, end_grad, weights_out, images_out, biases_out, end_out, sems
):
    pairs = [(weights, weights_out), (images, images_out), (biases, biases_out)]
    pairs.append((end_grad, end_out))
    copies = [pltpu.make_async_copy(a, b, sems.at[at]) for at, (a, b) in enumerate(pairs)]
    for copy in copies:
        copy.start()
    for copy in copies:
        copy.wait()


def flip_body(weights, transposed):
    taps, channels = weights.shape[1], weights.shape[2]
    for index in range(weights.shape[0]):
        for tap in range(taps):
            flipped = weights[index, taps - 1 - tap].astype(f32).T
            transposed[index, tap * channels : (tap + 1) * channels] = flipped.astype(bf16)


def start_body(images, own, before, weights, biases, payload, ref):
    clear_border(ref)
    field = images[...]
    state = field + times(field, before[...])
    for index in range(weights.shape[0]):
        state = state + 0.25 * jnp.tanh(
            convolve(ref, state, weights.at[index]) + biases[index : index + 1]
        )
    matrix = own[...]
    residual = state - (field + times(field, matrix))
    part = residual.shape[0] // GROUP
    for index in range(GROUP):
        payload[index, :part] = residual[index * part : (index + 1) * part]
        payload[index, part:] = matrix


def ends_body(images, end_grad, own, before, after, starts_out, ends_out, back_out):
    field = images[...]
    starts_out[...] = field + times(field, before[...])
    field = end_grad[...]
    ends_out[...] = field + times(field, after[...], True)
    back_out[...] = field + times(field, own[...], True)


def total_body(pieces, payload, locals_out):
    part = locals_out.shape[1]
    error = pieces[0, :part]
    product = pieces[0, part:]
    for index in range(1, GROUP):
        matrix = pieces[index, part:]
        locals_out[index] = error
        error = error + (times(error, matrix) + pieces[index, :part])
        product = product + (matrix + times(product, matrix))
    payload[:part] = error
    payload[part:] = product


def pair_body(part, spot, mine, theirs, out):
    upper = spot[1] == 1
    early = jnp.where(upper, theirs[...], mine[...])
    late = jnp.where(upper, mine[...], theirs[...])
    out[...] = early + (times(early, late[part:]) + late)


def back_pair_body(part, spot, mine, theirs, mine_full, theirs_full, out):
    upper = spot[1] == 1
    early = jnp.where(upper, mine[...], theirs[...])
    late = jnp.where(upper, theirs[...], mine[...])
    matrix = jnp.where(upper, theirs_full[part:], mine_full[part:])
    out[...] = early + (times(early, matrix, True) + late)


def products_body(part, pieces, prefix_out, suffix_out):
    before = pieces[0, part:]
    after = pieces[GROUP - 1, part:]
    for index in range(1, GROUP):
        prefix_out[index] = before
        suffix_out[GROUP - 1 - index] = after
        if index < GROUP - 1:
            matrix = pieces[index, part:]
            before = before + (matrix + times(before, matrix))
            matrix = pieces[GROUP - 1 - index, part:]
            after = after + (matrix + times(matrix, after))


def back_total_body(part, pieces, first, payload, locals_out):
    error = pieces[GROUP - 1]
    for index in range(GROUP - 2, -1, -1):
        locals_out[index] = error
        error = error + (times(error, first[index, part:], True) + pieces[index])
    payload[...] = error


def replay_body(
    spot, theirs, far1, far2, far3, locals_in, prefix_in, result, prefix, out, sem, sems
):
    stores = [pltpu.make_async_copy(out.at[at], result.at[at], sems.at[at]) for at in range(GROUP)]
    copy = pltpu.make_async_copy(prefix_in, prefix, sem)
    copy.start()
    part = out.shape[1]
    error = jnp.where(spot[0] >= 3, far3[:part], 0.0)
    for distance, group in ((2, far2), (1, far1)):
        longer = error + (times(error, group[part:]) + group[:part])
        error = jnp.where(spot[0] >= distance, longer, error)
    longer = error + (times(error, theirs[part:]) + theirs[:part])
    error = jnp.where(spot[1] == 1, longer, error)
    out[0] = error
    stores[0].start()
    copy.wait()
    for index in range(1, GROUP):
        out[index] = error + (times(error, prefix[index]) + locals_in[index])
        stores[index].start()
    for store in stores:
        store.wait()


def back_replay_body(
    spot, theirs, far1, far2, far3, theirs_full, full1, full2, locals_in, suffix_in,
    result, suffix, out, sem, sems,
):
    stores = [pltpu.make_async_copy(out.at[at], result.at[at], sems.at[at]) for at in range(GROUP)]
    copy = pltpu.make_async_copy(suffix_in, suffix, sem)
    copy.start()
    part = out.shape[1]
    error = far3[...]
    for group, full in ((far2, full2), (far1, full1)):
        error = error + (times(error, full[part:], True) + group[...])
    longer = error + (times(error, theirs_full[part:], True) + theirs[...])
    error = jnp.where(spot[1] == 0, longer, error)
    out[GROUP - 1] = error
    stores[GROUP - 1].start()
    copy.wait()
    for index in range(GROUP - 1):
        out[index] = error + (times(error, suffix[index], True) + locals_in[index])
        stores[index].start()
    for store in stores:
        store.wait()


def forward_sweep(state, weights, biases, ref, inputs, slopes, stores, fetches=None):
    for index in range(weights.shape[0]):
        if fetches is not None:
            fetches[index].wait()
        activation = jnp.tanh(convolve(ref, state, weights.at[index]) + biases[index : index + 1])
        channels = state.shape[1]
        inputs[index] = ref[:, :, :, channels : 2 * channels]
        slopes[index] = 0.25 * (1.0 - activation * activation)
        for store in stores[index]:
            store.start()
        state = state + 0.25 * activation
    return state


def sweep_stores(inputs, slopes, inputs_out, slopes_out, sems):
    blocks = inputs.shape[0]
    return [
        [
            pltpu.make_async_copy(inputs.at[index], inputs_out.at[index], sems.at[index]),
            pltpu.make_async_copy(slopes.at[index], slopes_out.at[index], sems.at[blocks + index]),
        ]
        for index in range(blocks)
    ]


def middle_body(
    corrected, ends_in, back_in, weights_in, transposed_in, biases_in,
    ends_out, inputs_out, slopes_out, residual_out,
    ref, ends, inputs, slopes, ends_adj, back, weights, transposed, biases, sems, loads,
):
    blocks = weights.shape[0]
    pairs = [(biases_in, biases)]
    pairs += [(weights_in.at[index], weights.at[index]) for index in range(blocks)]
    pairs += [(transposed_in, transposed), (ends_in, ends_adj), (back_in, back)]
    fetches = [pltpu.make_async_copy(a, b, loads.at[at]) for at, (a, b) in enumerate(pairs)]
    for fetch in fetches:
        fetch.start()
    clear_border(ref)
    stores = sweep_stores(inputs, slopes, inputs_out, slopes_out, sems)
    fetches[0].wait()
    ends[...] = forward_sweep(
        corrected[...], weights, biases, ref, inputs, slopes, stores, fetches[1 : 1 + blocks]
    )
    for fetch in fetches[1 + blocks :]:
        fetch.wait()
    last = pltpu.make_async_copy(ends, ends_out, sems.at[2 * blocks])
    last.start()
    adjoint = ends_adj[...]
    for index in reversed(range(blocks)):
        change = slopes[index] * adjoint
        adjoint = adjoint + convolve(ref, change, transposed.at[index])
    residual_out[...] = adjoint - back[...]
    for store in sum(stores, [last]):
        store.wait()


def again_body(corrected, weights, biases, inputs_out, slopes_out, ref, inputs, slopes, sems):
    clear_border(ref)
    stores = sweep_stores(inputs, slopes, inputs_out, slopes_out, sems)
    forward_sweep(corrected[...], weights, biases, ref, inputs, slopes, stores)
    for store in sum(stores, []):
        store.wait()


def finish_block(scale, adjoint, transposed, inputs, slope, ref):
    channels = adjoint.shape[1]
    change = slope * adjoint
    adjoint = adjoint + convolve(ref, change, transposed)
    offset = jnp.sum(change, axis=0, keepdims=True) * scale
    moved = rows_from(ref, 1)
    field = jnp.concatenate([rows_from(inputs, row_at) for row_at in range(3)], axis=1)
    kernel = scale * lax.dot_general(
        field, moved, (((0,), (0,)), ((), ())), preferred_element_type=f32
    )
    taps = [
        kernel[
            row_at * channels : (row_at + 1) * channels,
            (2 - col_at) * channels : (3 - col_at) * channels,
        ]
        for row_at in range(3)
        for col_at in range(3)
    ]
    taps.append(jnp.broadcast_to(offset, (EXTRA, channels)))
    return adjoint, jnp.concatenate(taps, axis=0)


def final_body(scale, moving, transposed, inputs, slopes, adjoint_out, kernels_out, ref):
    clear_border(ref)
    adjoint = moving[...]
    for index in reversed(range(transposed.shape[0])):
        adjoint, kernels_out[index] = finish_block(
            scale, adjoint, transposed.at[index], inputs.at[index], slopes[index], ref
        )
    adjoint_out[...] = adjoint


def other_body(
    scale, first, last, moving, transposed, inputs, slopes, kernels, adjoint_out, kernels_out, ref
):
    clear_border(ref)
    adjoint = moving[...]
    for index in reversed(range(first, last)):
        adjoint, kernel = finish_block(
            scale, adjoint, transposed.at[index], inputs.at[index], slopes[index], ref
        )
        kernels_out[index - first] = kernels[index] + kernel
    if adjoint_out is not None:
        adjoint_out[...] = adjoint


def join_body(first, mine, theirs, late, kernels_out, offsets_out, total, offsets, sems):
    size = kernels_out.shape[1]
    count = mine.shape[0]
    offsets[:count] = mine[:, size] + theirs[:, size]
    if late is not None:
        offsets[count:] = late[...]
    copies = [pltpu.make_async_copy(offsets, offsets_out, sems.at[count])]
    copies[0].start()
    for index in range(count):
        total[index] = mine[index, :size] + theirs[index, :size]
        copies.append(
            pltpu.make_async_copy(total.at[index], kernels_out.at[first + index], sems.at[index])
        )
        copies[-1].start()
    for copy in copies:
        copy.wait()


def shards(images, weights, biases, end_grad):
    count, height, width, channels = images.shape
    blocks = weights.shape[0]
    rows = count * height * width
    part = rows // GROUP
    layers = lax.axis_size("layer")
    outer = layers // GROUP
    near = [[a * GROUP + b for b in range(GROUP)] for a in range(outer)]
    pair = [(i, i ^ GROUP) for i in range(layers)]
    around = [[(i, (i + 2 * GROUP * d) % layers) for i in range(layers)] for d in (1, 2, 3)]
    down = [[(i, i - 2 * GROUP * d) for i in range(2 * GROUP * d, layers)] for d in (1, 2, 3)]
    dp = lax.axis_size("dp")
    partner = [(i, (i + dp // 2) % dp) for i in range(dp)]
    sibling = [(i, i ^ 1) for i in range(dp)]
    spot = lax.axis_index("layer").astype(jnp.int32)
    spot = jnp.stack([spot >> 4, (spot >> 3) & 1])
    scale = 1.0 / (count * dp)
    per_conv = 2 * rows * 9 * channels * channels
    half = blocks // 2

    def exchange(value, groups):
        return lax.all_to_all(value, "layer", 0, 0, axis_index_groups=groups)

    plane = shape((rows, channels))
    kept = stored((rows, channels))
    matrix = shape((channels, channels))
    pieces_shape = shape((GROUP, part, channels))
    pieces_kept = stored((GROUP, part, channels))
    both_kept = stored((GROUP, part + channels, channels))
    both = shape((part + channels, channels))
    piece = shape((part, channels))
    matrices = stored((GROUP, channels, channels))
    taps_shape = shape((blocks, 9, channels, channels), bf16)
    sweep_shape = (blocks, 9 * channels, channels)
    inputs_dims = (blocks, count, height + 2, width, channels)
    slopes_dims = (blocks, rows, channels)
    offsets_shape = shape((blocks, channels))
    kernels_shape = shape((blocks, 9 * channels + EXTRA, channels))
    half_kernels = shape((half, 9 * channels + EXTRA, channels))
    result = jax.ShapeDtypeStruct((rows, channels), f32)
    gradients = jax.ShapeDtypeStruct((blocks, 9 * channels, channels), f32)
    half_offsets = jax.ShapeDtypeStruct((half, channels), f32)
    ref = pltpu.VMEM((count, height + 2, width, 3 * channels), bf16)
    dma = pltpu.SemaphoreType.DMA
    sweep_scratch = [pltpu.VMEM(inputs_dims, bf16), pltpu.VMEM(slopes_dims, f32)]

    flat = weights.reshape(blocks, 9, channels, channels)
    kernels = weights.reshape(sweep_shape)
    (own,) = call(
        coarse_body, [matrix], in_hbm(flat), ins=[HBM],
        scratch=[pltpu.VMEM((blocks, channels, channels), bf16), dma(())], name="coarse",
    )
    before = lax.ppermute(own, "layer", [(i, i + 1) for i in range(layers - 1)])
    after = lax.ppermute(own, "layer", [(i + 1, i) for i in range(layers - 1)])
    held, field, offsets, cotangent = call(
        load_body, [taps_shape, plane, offsets_shape, plane],
        in_hbm(flat), in_hbm(images.reshape(rows, channels)), in_hbm(biases),
        in_hbm(end_grad.reshape(rows, channels)),
        ins=[HBM] * 4, scratch=[dma((4,))], name="load",
    )

    (payload,) = call(
        start_body, [both_kept], field, own, before, held.reshape(sweep_shape), offsets,
        scratch=[ref], flops=blocks * per_conv, name="start",
    )
    first = exchange(payload, near)
    first, after = lax.optimization_barrier((first, after))
    starts, ends_adj, back = call(
        ends_body, [kept] * 3, field, cotangent, own, before, after, name="ends"
    )
    (transposed,) = call(flip_body, [stored(sweep_shape, bf16)], flat, name="flip")
    first, transposed = lax.optimization_barrier((first, transposed))
    full, prefixes = call(total_body, [both, pieces_shape], first, name="total")
    their_full = lax.ppermute(full, "layer", pair)
    (pair_full,) = call(
        lambda *refs: pair_body(part, *refs), [both], spot, full, their_full,
        ins=[SMEM, VMEM, VMEM], name="pair",
    )
    around_full = [lax.ppermute(pair_full, "layer", to) for to in around]
    prefix, suffix = call(
        lambda *refs: products_body(part, *refs), [matrices] * 2, first, name="products"
    )
    replay_scratch = [
        pltpu.VMEM((GROUP, channels, channels), f32), pltpu.VMEM((GROUP, part, channels), f32),
        dma(()), dma((GROUP,)),
    ]
    (error,) = call(
        replay_body, [pieces_kept], spot, their_full, *around_full, prefixes, in_hbm(prefix),
        ins=[SMEM] + [VMEM] * 5 + [HBM], out_specs=[HBM], scratch=replay_scratch, name="replay",
    )
    error, suffix, starts, ends_adj, back = lax.optimization_barrier(
        (error, suffix, starts, ends_adj, back)
    )
    corrected = starts + exchange(error, near).reshape(rows, channels)
    other_corrected = lax.ppermute(corrected, "dp", partner)

    interval_ends, inputs, slopes, adj_residual = call(
        middle_body, [result, stored(inputs_dims, bf16), stored(slopes_dims), kept],
        corrected, in_hbm(ends_adj), in_hbm(back), in_hbm(kernels),
        in_hbm(transposed), in_hbm(biases),
        ins=[VMEM] + [HBM] * 5, out_specs=[HBM, HBM, HBM, VMEM],
        scratch=[ref, pltpu.VMEM((rows, channels), f32)] + sweep_scratch
        + [pltpu.VMEM((rows, channels), f32)] * 2 + [pltpu.VMEM(sweep_shape, bf16)] * 2
        + [pltpu.VMEM((blocks, channels), f32), dma((2 * blocks + 1,)), dma((blocks + 4,))],
        flops=2 * blocks * per_conv, name="middle",
    )
    pieces = exchange(adj_residual.reshape(GROUP, part, channels), near)
    total, prefixes = call(
        lambda *refs: back_total_body(part, *refs), [piece, pieces_shape], pieces, first,
        name="back_total",
    )
    their_total = lax.ppermute(total, "layer", pair)
    (pair_total,) = call(
        lambda *refs: back_pair_body(part, *refs), [piece],
        spot, total, their_total, full, their_full, ins=[SMEM] + [VMEM] * 4, name="back_pair",
    )
    down_total = [lax.ppermute(pair_total, "layer", to) for to in down]
    other_inputs, other_slopes = call(
        again_body, [stored(inputs_dims, bf16), stored(slopes_dims)],
        other_corrected, kernels, offsets, out_specs=[HBM] * 2,
        scratch=[ref] + sweep_scratch + [dma((2 * blocks,))], flops=blocks * per_conv, name="again",
    )
    (adj_error,) = call(
        back_replay_body, [pieces_kept], spot, their_total, *down_total, their_full,
        around_full[2], around_full[1], prefixes, in_hbm(suffix),
        ins=[SMEM] + [VMEM] * 8 + [HBM], out_specs=[HBM], scratch=replay_scratch,
        name="back_replay",
    )
    adj_error, other_inputs, other_slopes = lax.optimization_barrier(
        (adj_error, other_inputs, other_slopes)
    )
    moving = ends_adj + exchange(adj_error, near).reshape(rows, channels)
    other_moving = lax.ppermute(moving, "dp", partner)
    adjoint, kernel_part = call(
        lambda *refs: final_body(scale, *refs), [result, kernels_shape],
        moving, transposed, inputs, slopes,
        scratch=[ref], flops=2 * blocks * per_conv, name="final",
    )
    other_moving, late = call(
        lambda *refs: other_body(scale, half, blocks, *refs), [plane, half_kernels],
        other_moving, transposed, other_inputs, other_slopes, kernel_part,
        scratch=[ref], flops=blocks * per_conv, name="other_late",
    )
    their_late = lax.ppermute(late, "dp", sibling)
    (early,) = call(
        lambda moving, a, b, c, d, out, ref: other_body(
            scale, 0, half, moving, a, b, c, d, None, out, ref
        ),
        [half_kernels], other_moving, transposed, other_inputs, other_slopes, kernel_part,
        scratch=[ref], flops=blocks * per_conv, name="other_early",
    )
    their_early = lax.ppermute(early, "dp", sibling)
    sums = pltpu.VMEM((half, 9 * channels, channels), f32)
    weight_grad, late_offsets = call(
        lambda mine, theirs, *refs: join_body(half, mine, theirs, None, *refs),
        [gradients, half_offsets], late, their_late,
        out_specs=[HBM, HBM], name="join_late",
        scratch=[sums, pltpu.VMEM((half, channels), f32), dma((half + 1,))],
    )
    weight_grad, bias_grad = call(
        lambda mine, theirs, offsets, _, *refs: join_body(0, mine, theirs, offsets, *refs),
        [gradients, jax.ShapeDtypeStruct((blocks, channels), f32)],
        early, their_early, late_offsets, weight_grad,
        ins=[VMEM, VMEM, VMEM, HBM], out_specs=[HBM, HBM], aliases={3: 0}, name="join_early",
        scratch=[sums, pltpu.VMEM((blocks, channels), f32), dma((half + 1,))],
    )
    dims = (1, count, height, width, channels)
    return (
        interval_ends.reshape(dims),
        adjoint.reshape(dims),
        weight_grad.reshape(blocks, 3, 3, channels, channels),
        bias_grad,
    )


def solution(mesh):
    in_specs = (
        P("dp", None, None, None),
        P("layer", None, None, None, None),
        P("layer", None),
        P("dp", None, None, None),
    )
    out_specs = (
        P("layer", "dp", None, None, None),
        P("layer", "dp", None, None, None),
        P("layer", None, None, None, None),
        P("layer", None),
    )
    return jax.shard_map(shards, mesh=mesh, in_specs=in_specs, out_specs=out_specs, check_vma=False)
```

```python
import math

import jax
import jax.numpy as jnp
from jax import lax
from jax.experimental import pallas as pl
from jax.experimental.pallas import tpu as pltpu
from jax.sharding import PartitionSpec as P

GROUP = 8
EXTRA = 8
VMEM_LIMIT = 12 * 1024 * 1024
f32 = jnp.float32
bf16 = jnp.bfloat16


def shifted_columns(value, width):
    rows = value.shape[0]
    at = lax.broadcasted_iota(jnp.int32, value.shape, 0) % width
    left = jnp.where(at == 0, 0.0, pltpu.roll(value, 1, 0))
    right = jnp.where(at == width - 1, 0.0, pltpu.roll(value, rows - 1, 0))
    return jnp.concatenate([left.astype(bf16), value.astype(bf16), right.astype(bf16)], axis=1)


def clear_border(ref):
    height = ref.shape[1]
    edge = jnp.zeros((ref.shape[0], 1) + ref.shape[2:], ref.dtype)
    ref[:, 0:1] = edge
    ref[:, height - 1 : height] = edge


def rows_from(ref, row_at):
    images, height, width, lanes = ref.shape
    return ref[:, row_at : row_at + height - 2].reshape(images * (height - 2) * width, lanes)


def convolve(ref, value, kernel):
    images, height, width, lanes = ref.shape
    rows = (height - 2) * width
    parts = []
    for image in range(images):
        moved = shifted_columns(value[image * rows : (image + 1) * rows], width)
        ref[image, 1 : height - 1] = moved.reshape(height - 2, width, lanes)
        window = [ref[image, at : at + height - 2].reshape(rows, lanes) for at in range(3)]
        parts.append(
            jnp.dot(jnp.concatenate(window, axis=1), kernel[...], preferred_element_type=f32)
        )
    return jnp.concatenate(parts, axis=0)


def split(value):
    high = value.astype(bf16)
    low = (value - high.astype(f32)).astype(bf16)
    return high, low


def times(value, matrix, transpose=False):
    dims = (((1,), (1 if transpose else 0,)), ((), ()))
    high, low = split(value)
    mhigh, mlow = split(matrix)
    dot = lambda a, b: lax.dot_general(a, b, dims, preferred_element_type=f32)
    rows = value.shape[0]
    both = dot(jnp.concatenate([high, low], axis=0), mhigh)
    return both[:rows] + (both[rows:] + dot(high, mlow))


VMEM = pl.BlockSpec(memory_space=pltpu.VMEM)
SMEM = pl.BlockSpec(memory_space=pltpu.SMEM)
HBM = pl.BlockSpec(memory_space=pltpu.HBM)


def call(body, outs, *args, ins=None, out_specs=None, scratch=(), flops=0, aliases=None, name=None):
    size = sum(a.size * a.dtype.itemsize for a in args)
    size += sum(math.prod(o.shape) * jnp.dtype(o.dtype).itemsize for o in outs)
    return pl.pallas_call(
        body,
        out_shape=tuple(outs),
        in_specs=list(ins) if ins else [VMEM] * len(args),
        out_specs=tuple(out_specs) if out_specs else (VMEM,) * len(outs),
        scratch_shapes=list(scratch),
        input_output_aliases=aliases or {},
        cost_estimate=pl.CostEstimate(flops=flops, bytes_accessed=size, transcendentals=0),
        compiler_params=pltpu.CompilerParams(vmem_limit_bytes=VMEM_LIMIT),
        name=name,
    )(*args)


def shape(dims, dtype=f32):
    return pltpu.VMEM(dims, dtype)


def stored(dims, dtype=f32):
    return pltpu.HBM(dims, dtype)


def in_hbm(value):
    return pltpu.with_memory_space_constraint(value, pltpu.HBM)


def coarse_body(weights, out, centre, sem):
    copy = pltpu.make_async_copy(weights.at[:, 4], centre, sem)
    copy.start()
    copy.wait()
    total = centre[0].astype(f32)
    for index in range(1, centre.shape[0]):
        total = total + centre[index].astype(f32)
    out[...] = 0.25 * total


def load_body(
    weights, images, biases, end_grad, weights_out, images_out, biases_out, end_out, sems
):
    pairs = [(weights, weights_out), (images, images_out), (biases, biases_out)]
    pairs.append((end_grad, end_out))
    copies = [pltpu.make_async_copy(a, b, sems.at[at]) for at, (a, b) in enumerate(pairs)]
    for copy in copies:
        copy.start()
    for copy in copies:
        copy.wait()


def flip_body(weights, transposed):
    taps, channels = weights.shape[1], weights.shape[2]
    for index in range(weights.shape[0]):
        for tap in range(taps):
            flipped = weights[index, taps - 1 - tap].astype(f32).T
            transposed[index, tap * channels : (tap + 1) * channels] = flipped.astype(bf16)


def start_body(images, own, before, weights, biases, payload, ref):
    clear_border(ref)
    field = images[...]
    state = field + times(field, before[...])
    for index in range(weights.shape[0]):
        state = state + 0.25 * jnp.tanh(
            convolve(ref, state, weights.at[index]) + biases[index : index + 1]
        )
    matrix = own[...]
    residual = state - (field + times(field, matrix))
    part = residual.shape[0] // GROUP
    for index in range(GROUP):
        payload[index, :part] = residual[index * part : (index + 1) * part]
        payload[index, part:] = matrix


def ends_body(images, end_grad, own, before, after, starts_out, ends_out, back_out):
    field = images[...]
    starts_out[...] = field + times(field, before[...])
    field = end_grad[...]
    ends_out[...] = field + times(field, after[...], True)
    back_out[...] = field + times(field, own[...], True)


def total_body(pieces, payload, locals_out):
    part = locals_out.shape[1]
    error = pieces[0, :part]
    product = pieces[0, part:]
    for index in range(1, GROUP):
        matrix = pieces[index, part:]
        locals_out[index] = error
        error = error + (times(error, matrix) + pieces[index, :part])
        product = product + (matrix + times(product, matrix))
    payload[:part] = error
    payload[part:] = product


def pair_body(part, spot, mine, theirs, out):
    upper = spot[1] == 1
    early = jnp.where(upper, theirs[...], mine[...])
    late = jnp.where(upper, mine[...], theirs[...])
    out[...] = early + (times(early, late[part:]) + late)


def back_pair_body(part, spot, mine, theirs, mine_full, theirs_full, out):
    upper = spot[1] == 1
    early = jnp.where(upper, mine[...], theirs[...])
    late = jnp.where(upper, theirs[...], mine[...])
    matrix = jnp.where(upper, theirs_full[part:], mine_full[part:])
    out[...] = early + (times(early, matrix, True) + late)


def products_body(part, pieces, prefix_out, suffix_out):
    before = pieces[0, part:]
    after = pieces[GROUP - 1, part:]
    for index in range(1, GROUP):
        prefix_out[index] = before
        suffix_out[GROUP - 1 - index] = after
        if index < GROUP - 1:
            matrix = pieces[index, part:]
            before = before + (matrix + times(before, matrix))
            matrix = pieces[GROUP - 1 - index, part:]
            after = after + (matrix + times(matrix, after))


def back_total_body(part, pieces, first, payload, locals_out):
    error = pieces[GROUP - 1]
    for index in range(GROUP - 2, -1, -1):
        locals_out[index] = error
        error = error + (times(error, first[index, part:], True) + pieces[index])
    payload[...] = error


def replay_body(
    spot, theirs, far1, far2, far3, locals_in, prefix_in, result, prefix, out, sem, sems
):
    stores = [pltpu.make_async_copy(out.at[at], result.at[at], sems.at[at]) for at in range(GROUP)]
    copy = pltpu.make_async_copy(prefix_in, prefix, sem)
    copy.start()
    part = out.shape[1]
    error = jnp.where(spot[0] >= 3, far3[:part], 0.0)
    for distance, group in ((2, far2), (1, far1)):
        longer = error + (times(error, group[part:]) + group[:part])
        error = jnp.where(spot[0] >= distance, longer, error)
    longer = error + (times(error, theirs[part:]) + theirs[:part])
    error = jnp.where(spot[1] == 1, longer, error)
    out[0] = error
    stores[0].start()
    copy.wait()
    for index in range(1, GROUP):
        out[index] = error + (times(error, prefix[index]) + locals_in[index])
        stores[index].start()
    for store in stores:
        store.wait()


def back_replay_body(
    spot, theirs, far1, far2, far3, theirs_full, full1, full2, locals_in, suffix_in,
    result, suffix, out, sem, sems,
):
    stores = [pltpu.make_async_copy(out.at[at], result.at[at], sems.at[at]) for at in range(GROUP)]
    copy = pltpu.make_async_copy(suffix_in, suffix, sem)
    copy.start()
    part = out.shape[1]
    error = far3[...]
    for group, full in ((far2, full2), (far1, full1)):
        error = error + (times(error, full[part:], True) + group[...])
    longer = error + (times(error, theirs_full[part:], True) + theirs[...])
    error = jnp.where(spot[1] == 0, longer, error)
    out[GROUP - 1] = error
    stores[GROUP - 1].start()
    copy.wait()
    for index in range(GROUP - 1):
        out[index] = error + (times(error, suffix[index], True) + locals_in[index])
        stores[index].start()
    for store in stores:
        store.wait()


def forward_sweep(state, weights, biases, ref, inputs, slopes, stores, fetches=None):
    for index in range(weights.shape[0]):
        preact = convolve(ref, state, weights.at[index])
        if fetches is not None and index == 0:
            fetches[0].wait()
        activation = jnp.tanh(preact + biases[index : index + 1])
        channels = state.shape[1]
        inputs[index] = ref[:, :, :, channels : 2 * channels]
        slopes[index] = 0.25 * (1.0 - activation * activation)
        for store in stores[index]:
            store.start()
        state = state + 0.25 * activation
    return state


def sweep_stores(inputs, slopes, inputs_out, slopes_out, sems):
    blocks = inputs.shape[0]
    return [
        [
            pltpu.make_async_copy(inputs.at[index], inputs_out.at[index], sems.at[index]),
            pltpu.make_async_copy(slopes.at[index], slopes_out.at[index], sems.at[blocks + index]),
        ]
        for index in range(blocks)
    ]


def middle_body(
    corrected, weights, ends_in, back_in, transposed_in, biases_in,
    ends_out, inputs_out, slopes_out, residual_out,
    ref, ends, inputs, slopes, ends_adj, back, transposed, biases, sems, loads,
):
    blocks = weights.shape[0]
    pairs = [(biases_in, biases)]
    pairs += [(transposed_in, transposed), (ends_in, ends_adj), (back_in, back)]
    fetches = [pltpu.make_async_copy(a, b, loads.at[at]) for at, (a, b) in enumerate(pairs)]
    for fetch in fetches:
        fetch.start()
    clear_border(ref)
    stores = sweep_stores(inputs, slopes, inputs_out, slopes_out, sems)
    ends[...] = forward_sweep(
        corrected[...], weights, biases, ref, inputs, slopes, stores, fetches[:1]
    )
    for fetch in fetches[1:]:
        fetch.wait()
    last = pltpu.make_async_copy(ends, ends_out, sems.at[2 * blocks])
    last.start()
    adjoint = ends_adj[...]
    for index in reversed(range(blocks)):
        change = slopes[index] * adjoint
        adjoint = adjoint + convolve(ref, change, transposed.at[index])
    residual_out[...] = adjoint - back[...]
    for store in sum(stores, [last]):
        store.wait()


def again_body(corrected, weights, biases, inputs_out, slopes_out, ref, inputs, slopes, sems):
    clear_border(ref)
    stores = sweep_stores(inputs, slopes, inputs_out, slopes_out, sems)
    forward_sweep(corrected[...], weights, biases, ref, inputs, slopes, stores)
    for store in sum(stores, []):
        store.wait()


def finish_block(scale, adjoint, transposed, inputs, slope, ref):
    channels = adjoint.shape[1]
    change = slope * adjoint
    adjoint = adjoint + convolve(ref, change, transposed)
    offset = jnp.sum(change, axis=0, keepdims=True) * scale
    moved = rows_from(ref, 1)
    field = jnp.concatenate([rows_from(inputs, row_at) for row_at in range(3)], axis=1)
    kernel = scale * lax.dot_general(
        field, moved, (((0,), (0,)), ((), ())), preferred_element_type=f32
    )
    taps = [
        kernel[
            row_at * channels : (row_at + 1) * channels,
            (2 - col_at) * channels : (3 - col_at) * channels,
        ]
        for row_at in range(3)
        for col_at in range(3)
    ]
    taps.append(jnp.broadcast_to(offset, (EXTRA, channels)))
    return adjoint, jnp.concatenate(taps, axis=0)


def final_body(scale, moving, transposed, inputs, slopes, adjoint_out, kernels_out, ref):
    clear_border(ref)
    adjoint = moving[...]
    for index in reversed(range(transposed.shape[0])):
        adjoint, kernels_out[index] = finish_block(
            scale, adjoint, transposed.at[index], inputs.at[index], slopes[index], ref
        )
    adjoint_out[...] = adjoint


def other_body(
    scale, first, last, moving, transposed, inputs, slopes, kernels, adjoint_out, kernels_out, ref
):
    clear_border(ref)
    adjoint = moving[...]
    for index in reversed(range(first, last)):
        adjoint, kernel = finish_block(
            scale, adjoint, transposed.at[index], inputs.at[index], slopes[index], ref
        )
        kernels_out[index - first] = kernels[index] + kernel
    if adjoint_out is not None:
        adjoint_out[...] = adjoint


def join_body(first, mine, theirs, late, kernels_out, offsets_out, total, offsets, sems):
    size = kernels_out.shape[1]
    count = mine.shape[0]
    offsets[:count] = mine[:, size] + theirs[:, size]
    if late is not None:
        offsets[count:] = late[...]
    copies = [pltpu.make_async_copy(offsets, offsets_out, sems.at[count])]
    copies[0].start()
    for index in range(count):
        total[index] = mine[index, :size] + theirs[index, :size]
        copies.append(
            pltpu.make_async_copy(total.at[index], kernels_out.at[first + index], sems.at[index])
        )
        copies[-1].start()
    for copy in copies:
        copy.wait()


def shards(images, weights, biases, end_grad):
    count, height, width, channels = images.shape
    blocks = weights.shape[0]
    rows = count * height * width
    part = rows // GROUP
    layers = lax.axis_size("layer")
    outer = layers // GROUP
    near = [[a * GROUP + b for b in range(GROUP)] for a in range(outer)]
    pair = [(i, i ^ GROUP) for i in range(layers)]
    around = [[(i, (i + 2 * GROUP * d) % layers) for i in range(layers)] for d in (1, 2, 3)]
    down = [[(i, i - 2 * GROUP * d) for i in range(2 * GROUP * d, layers)] for d in (1, 2, 3)]
    dp = lax.axis_size("dp")
    partner = [(i, (i + dp // 2) % dp) for i in range(dp)]
    sibling = [(i, i ^ 1) for i in range(dp)]
    spot = lax.axis_index("layer").astype(jnp.int32)
    spot = jnp.stack([spot >> 4, (spot >> 3) & 1])
    scale = 1.0 / (count * dp)
    per_conv = 2 * rows * 9 * channels * channels
    half = blocks // 2

    def exchange(value, groups):
        return lax.all_to_all(value, "layer", 0, 0, axis_index_groups=groups)

    plane = shape((rows, channels))
    kept = stored((rows, channels))
    matrix = shape((channels, channels))
    pieces_shape = shape((GROUP, part, channels))
    pieces_kept = stored((GROUP, part, channels))
    both_kept = stored((GROUP, part + channels, channels))
    both = shape((part + channels, channels))
    piece = shape((part, channels))
    matrices = stored((GROUP, channels, channels))
    taps_shape = shape((blocks, 9, channels, channels), bf16)
    sweep_shape = (blocks, 9 * channels, channels)
    inputs_dims = (blocks, count, height + 2, width, channels)
    slopes_dims = (blocks, rows, channels)
    offsets_shape = shape((blocks, channels))
    kernels_shape = shape((blocks, 9 * channels + EXTRA, channels))
    half_kernels = shape((half, 9 * channels + EXTRA, channels))
    result = jax.ShapeDtypeStruct((rows, channels), f32)
    gradients = jax.ShapeDtypeStruct((blocks, 9 * channels, channels), f32)
    half_offsets = jax.ShapeDtypeStruct((half, channels), f32)
    ref = pltpu.VMEM((count, height + 2, width, 3 * channels), bf16)
    dma = pltpu.SemaphoreType.DMA
    sweep_scratch = [pltpu.VMEM(inputs_dims, bf16), pltpu.VMEM(slopes_dims, f32)]

    flat = weights.reshape(blocks, 9, channels, channels)
    kernels = weights.reshape(sweep_shape)
    (own,) = call(
        coarse_body, [matrix], in_hbm(flat), ins=[HBM],
        scratch=[pltpu.VMEM((blocks, channels, channels), bf16), dma(())], name="coarse",
    )
    before = lax.ppermute(own, "layer", [(i, i + 1) for i in range(layers - 1)])
    after = lax.ppermute(own, "layer", [(i + 1, i) for i in range(layers - 1)])
    held, field, offsets, cotangent = call(
        load_body, [taps_shape, plane, offsets_shape, plane],
        in_hbm(flat), in_hbm(images.reshape(rows, channels)), in_hbm(biases),
        in_hbm(end_grad.reshape(rows, channels)),
        ins=[HBM] * 4, scratch=[dma((4,))], name="load",
    )

    (payload,) = call(
        start_body, [both_kept], field, own, before, held.reshape(sweep_shape), offsets,
        scratch=[ref], flops=blocks * per_conv, name="start",
    )
    first = exchange(payload, near)
    first, after = lax.optimization_barrier((first, after))
    starts, ends_adj, back = call(
        ends_body, [kept] * 3, field, cotangent, own, before, after, name="ends"
    )
    (transposed,) = call(flip_body, [stored(sweep_shape, bf16)], flat, name="flip")
    first, transposed = lax.optimization_barrier((first, transposed))
    full, prefixes = call(total_body, [both, pieces_shape], first, name="total")
    their_full = lax.ppermute(full, "layer", pair)
    (pair_full,) = call(
        lambda *refs: pair_body(part, *refs), [both], spot, full, their_full,
        ins=[SMEM, VMEM, VMEM], name="pair",
    )
    around_full = [lax.ppermute(pair_full, "layer", to) for to in around]
    prefix, suffix = call(
        lambda *refs: products_body(part, *refs), [matrices] * 2, first, name="products"
    )
    replay_scratch = [
        pltpu.VMEM((GROUP, channels, channels), f32), pltpu.VMEM((GROUP, part, channels), f32),
        dma(()), dma((GROUP,)),
    ]
    (error,) = call(
        replay_body, [pieces_kept], spot, their_full, *around_full, prefixes, in_hbm(prefix),
        ins=[SMEM] + [VMEM] * 5 + [HBM], out_specs=[HBM], scratch=replay_scratch, name="replay",
    )
    error, suffix, starts, ends_adj, back = lax.optimization_barrier(
        (error, suffix, starts, ends_adj, back)
    )
    corrected = starts + exchange(error, near).reshape(rows, channels)
    other_corrected = lax.ppermute(corrected, "dp", partner)

    interval_ends, inputs, slopes, adj_residual = call(
        middle_body, [result, stored(inputs_dims, bf16), stored(slopes_dims), kept],
        corrected, kernels, in_hbm(ends_adj), in_hbm(back),
        in_hbm(transposed), in_hbm(biases),
        ins=[VMEM] * 2 + [HBM] * 4, out_specs=[HBM, HBM, HBM, VMEM],
        scratch=[ref, pltpu.VMEM((rows, channels), f32)] + sweep_scratch
        + [pltpu.VMEM((rows, channels), f32)] * 2 + [pltpu.VMEM(sweep_shape, bf16)]
        + [pltpu.VMEM((blocks, channels), f32), dma((2 * blocks + 1,)), dma((4,))],
        flops=2 * blocks * per_conv, name="middle",
    )
    pieces = exchange(adj_residual.reshape(GROUP, part, channels), near)
    total, prefixes = call(
        lambda *refs: back_total_body(part, *refs), [piece, pieces_shape], pieces, first,
        name="back_total",
    )
    their_total = lax.ppermute(total, "layer", pair)
    (pair_total,) = call(
        lambda *refs: back_pair_body(part, *refs), [piece],
        spot, total, their_total, full, their_full, ins=[SMEM] + [VMEM] * 4, name="back_pair",
    )
    down_total = [lax.ppermute(pair_total, "layer", to) for to in down]
    other_inputs, other_slopes = call(
        again_body, [stored(inputs_dims, bf16), stored(slopes_dims)],
        other_corrected, kernels, offsets, out_specs=[HBM] * 2,
        scratch=[ref] + sweep_scratch + [dma((2 * blocks,))], flops=blocks * per_conv, name="again",
    )
    (adj_error,) = call(
        back_replay_body, [pieces_kept], spot, their_total, *down_total, their_full,
        around_full[2], around_full[1], prefixes, in_hbm(suffix),
        ins=[SMEM] + [VMEM] * 8 + [HBM], out_specs=[HBM], scratch=replay_scratch,
        name="back_replay",
    )
    adj_error, other_inputs, other_slopes = lax.optimization_barrier(
        (adj_error, other_inputs, other_slopes)
    )
    moving = ends_adj + exchange(adj_error, near).reshape(rows, channels)
    other_moving = lax.ppermute(moving, "dp", partner)
    adjoint, kernel_part = call(
        lambda *refs: final_body(scale, *refs), [result, kernels_shape],
        moving, transposed, inputs, slopes,
        scratch=[ref], flops=2 * blocks * per_conv, name="final",
    )
    other_moving, late = call(
        lambda *refs: other_body(scale, half, blocks, *refs), [plane, half_kernels],
        other_moving, transposed, other_inputs, other_slopes, kernel_part,
        scratch=[ref], flops=blocks * per_conv, name="other_late",
    )
    their_late = lax.ppermute(late, "dp", sibling)
    (early,) = call(
        lambda moving, a, b, c, d, out, ref: other_body(
            scale, 0, half, moving, a, b, c, d, None, out, ref
        ),
        [half_kernels], other_moving, transposed, other_inputs, other_slopes, kernel_part,
        scratch=[ref], flops=blocks * per_conv, name="other_early",
    )
    their_early = lax.ppermute(early, "dp", sibling)
    sums = pltpu.VMEM((half, 9 * channels, channels), f32)
    weight_grad, late_offsets = call(
        lambda mine, theirs, *refs: join_body(half, mine, theirs, None, *refs),
        [gradients, half_offsets], late, their_late,
        out_specs=[HBM, HBM], name="join_late",
        scratch=[sums, pltpu.VMEM((half, channels), f32), dma((half + 1,))],
    )
    weight_grad, bias_grad = call(
        lambda mine, theirs, offsets, _, *refs: join_body(0, mine, theirs, offsets, *refs),
        [gradients, jax.ShapeDtypeStruct((blocks, channels), f32)],
        early, their_early, late_offsets, weight_grad,
        ins=[VMEM, VMEM, VMEM, HBM], out_specs=[HBM, HBM], aliases={3: 0}, name="join_early",
        scratch=[sums, pltpu.VMEM((blocks, channels), f32), dma((half + 1,))],
    )
    dims = (1, count, height, width, channels)
    return (
        interval_ends.reshape(dims),
        adjoint.reshape(dims),
        weight_grad.reshape(blocks, 3, 3, channels, channels),
        bias_grad,
    )


def solution(mesh):
    in_specs = (
        P("dp", None, None, None),
        P("layer", None, None, None, None),
        P("layer", None),
        P("dp", None, None, None),
    )
    out_specs = (
        P("layer", "dp", None, None, None),
        P("layer", "dp", None, None, None),
        P("layer", None, None, None, None),
        P("layer", None),
    )
    return jax.shard_map(shards, mesh=mesh, in_specs=in_specs, out_specs=out_specs, check_vma=False)
```
